32 devices in a mesh: dp: 2 (over y), seq: 8 (over z, x), head: 2 (over core).
Axes of the slice: x: 2, y: 2, z: 4, core: 2. Of those that a mesh axis runs over, the one named last changes fastest.
Arguments:
- queries: bfloat16 [128, 8, 1024], P('seq', 'dp', 'head'), parts along dimension 1, may hold values from -6 to 6
- gate_pre: bfloat16 [128, 8, 1024], P('seq', 'dp', 'head'), parts along dimension 1, may hold values from -6 to 6
- event_keys: bfloat16 [8192, 8, 1024], P('seq', 'dp', 'head'), parts along dimension 1, may hold values from -6 to 6
- event_values: bfloat16 [8192, 8, 1024], P('seq', 'dp', 'head'), parts along dimension 1, may hold values from -6 to 6
- block_lists: int32 [8, 8, 4], P(None, 'dp'), parts along dimension 1, may hold values from 0 to 7, all different within a row; in each aligned block of 4 rows (0 to 3, 4 to 7, ..., all dimensions but the last counted through in order) at most 2 rows name the same one
- history_len: int32 [8], P('dp'), parts along dimension 0, may hold values from 4 to 8
- out_grad: bfloat16 [128, 8, 1024], P('seq', 'dp', 'head'), parts along dimension 1, may hold values from -6 to 6
Outputs:
- layer_out: bfloat16 [128, 8, 1024], P('seq', 'dp', 'head'), parts along dimension 1
- grad_queries: bfloat16 [128, 8, 1024], P('seq', 'dp', 'head'), parts along dimension 1
- grad_gate: bfloat16 [128, 8, 1024], P('seq', 'dp', 'head'), parts along dimension 1
- grad_keys: bfloat16 [8192, 8, 1024], P('seq', 'dp', 'head'), parts along dimension 1
- grad_values: bfloat16 [8192, 8, 1024], P('seq', 'dp', 'head'), parts along dimension 1
The draws below stay inside these ranges and needn't reach their ends.
There are 2 independent parts, one for each index of `dp`. The reference program is written for one: setup_inputs(seed, part) draws one part's arguments, and reference() takes and returns one part's arrays. A program takes and returns all parts, laid end to end along the dimension named above; each array names one. Nothing has to cross between parts.
Inputs may be any that keep to these rules, and one draw needn't show every extreme that they name: Latent span c of user u names blocks (c - block_lists[c, u, i]) mod 8; the 4 entries of one row differ. Among the 4 rows of one latent span no offset occurs in more than 2 rows, and in some latent span one offset occurs in exactly 2 rows.
All inputs are finite; a program needn't handle non-finite values.
Results may differ from the reference program's by a relative error of at most 0.014.
Values may be sent and summed in bfloat16 or wider, within the bound.
A program may use at most 192 MiB of HBM per device.

```python
import math
import jax
import jax.numpy as jnp
import numpy as np
from jax import lax

HEADS = 16
HEAD_DIM = 64
D = 1024
USERS = 4
SPAN_ROWS = 16
BLOCK_ROWS = 1024
ENTRIES = 4
SLOTS = 2
LATENTS = 128
EVENTS = 8192
N_SEQ = 8


def plant(result, stream_key, low, high):
    longest = result.shape.index(max(result.shape))
    spots = []
    for shift in (0, 1):
        where = [jax.random.randint(jax.random.fold_in(stream_key, axis), (), 0, length) for axis, length in enumerate(result.shape)]
        where[longest] = (where[longest] + shift) % result.shape[longest]
        spots.append(tuple(where))
    return result.at[spots[0]].set(low).at[spots[1]].set(high)


def block_levels(own_key, extent, split, least, largest):
    level, own = 1.0, jax.random.fold_in(own_key, 6)
    for axis_at, shards_of in split:
        heights = jnp.exp(jax.random.uniform(jax.random.fold_in(own, axis_at), (shards_of,), jnp.float32, least / len(split), largest / len(split)))
        level = level * jnp.repeat(heights, extent[axis_at] // shards_of).reshape([-1 if axis == axis_at else 1 for axis in range(len(extent))])
    return level


def deal_out(rng, own, number, rows, amount, top, most, lean):
    ranking = jax.random.permutation(rng, amount)
    packed, ordinary = load_shares(amount, rows * top, most, lean, True), load_shares(amount, rows * top, most, lean, False)
    places = jnp.arange(amount)

    def named(tallies, offset_by):
        used = int((tallies > 0).sum())
        fixed = max(1, used // 4)
        shifted = fixed + (places - fixed + offset_by * (used - fixed)) % max(1, amount - fixed)
        return jnp.zeros((amount,), jnp.int32).at[ranking[jnp.where(places < fixed, places, shifted)]].set(jnp.asarray(tallies, jnp.int32))

    tallies = jnp.where(number % 4 == 0, named(packed, number // 4), named(ordinary, number - number // 4 - 1))
    mixed = jax.random.permutation(jax.random.fold_in(own, 3), amount)
    donor, taker = mixed[0:amount // 2 * 2:2], mixed[1:amount // 2 * 2:2]
    margin = jnp.minimum(tallies[donor] - 1, most - tallies[taker]) // 2
    margin = jnp.where((donor == ranking[0]) | (taker == ranking[0]) | (tallies[taker] == 0), 0, jnp.maximum(margin, 0))
    shifted = jax.random.randint(jax.random.fold_in(own, 4), (amount // 2,), 0, 1 << 20) % (margin + 1)
    tallies = tallies.at[donor].add(-shifted).at[taker].add(shifted)
    members = jnp.searchsorted(jnp.cumsum(tallies), jnp.arange(rows * top), side="right").astype(jnp.int32)
    grid = members.reshape(top, rows).T
    grid = grid[jax.random.permutation(jax.random.fold_in(own, 1), rows)]
    offset_by = jax.random.randint(jax.random.fold_in(own, 2), (rows, 1), 0, top)
    return jnp.take_along_axis(grid, (jnp.arange(top)[None, :] + offset_by) % top, axis=1)


def load_shares(number_of, total, bound, skew, full):
    portions = [(1 << 20) // math.isqrt(grade ** skew) + 1 for grade in range(1, number_of + 1)]
    largest = bound if full else min(bound, max(-(-total // number_of), total * portions[0] // sum(portions)))
    least = 1 if total - largest >= number_of - 1 else 0
    holding, surplus = [largest] + [least] * (number_of - 1), total - largest - least * (number_of - 1)
    while surplus > 0:
        movable = [i for i in range(1, number_of) if holding[i] < largest] or [i for i in range(1, number_of) if holding[i] < bound]
        whole, left = sum([portions[i] for i in movable]), surplus
        for i in movable:
            addition = min(bound - holding[i], max(1, left * portions[i] // whole), surplus)
            holding[i] = holding[i] + addition
            surplus = surplus - addition
    return np.array(holding)


def gaussian(own_key, dims, width, limit, shards=(), held_as=jnp.bfloat16):
    loudness = block_levels(own_key, dims, shards, -0.22, 0.18) if shards else 1.0
    array = jax.random.normal(own_key, dims, jnp.float32) * width * loudness
    return jnp.minimum(jnp.maximum(array, -limit), limit).astype(held_as)


def setup_inputs(seed: int = 0, part: int = 0) -> dict:
    streams_of = jax.random.split(jax.random.key(seed), 8)
    part_splits = jax.random.split(jax.random.fold_in(streams_of[7], part), 8)
    queries = gaussian(part_splits[0], (LATENTS, USERS, D), 1.0, 6.0, ((0, 8), (2, 2)))
    gate_pre = gaussian(part_splits[1], (LATENTS, USERS, D), 1.0, 6.0, ((0, 8), (2, 2)))
    event_keys = gaussian(part_splits[2], (EVENTS, USERS, D), 1.0, 6.0, ((0, 8), (2, 2)))
    event_values = gaussian(part_splits[3], (EVENTS, USERS, D), 1.0, 6.0, ((0, 8), (2, 2)))
    block_lists_keys = jax.random.split(jax.random.fold_in(part_splits[4], 1), N_SEQ * USERS // USERS)
    block_lists_turns = jax.random.permutation(jax.random.fold_in(part_splits[4], 3), N_SEQ * USERS // USERS)
    block_lists = jax.vmap(lambda own, number: deal_out(jax.random.fold_in(part_splits[4], 2), own, number, USERS, N_SEQ, ENTRIES, SLOTS, 2))(block_lists_keys, block_lists_turns).reshape((N_SEQ, USERS, ENTRIES))
    history_len = plant(jax.random.randint(part_splits[5], (USERS,), N_SEQ // 2, N_SEQ + 1), jax.random.fold_in(part_splits[5], 1), N_SEQ // 2, N_SEQ).astype(jnp.int32)
    out_grad = gaussian(part_splits[6], (LATENTS, USERS, D), 1.0, 6.0, ((0, 8), (2, 2)))
    return {"queries": queries, "gate_pre": gate_pre, "event_keys": event_keys, "event_values": event_values, "block_lists": block_lists, "history_len": history_len, "out_grad": out_grad}


EPS = 1e-06

def silu_slope(scores):
    logistic = jax.nn.sigmoid(scores)
    return logistic * (1.0 + scores * (1.0 - logistic))

def reference(queries, gate_pre, event_keys, event_values, block_lists, history_len, out_grad):
    factor = 1.0 / math.sqrt(HEAD_DIM)
    key_blocks = event_keys.reshape(N_SEQ, BLOCK_ROWS, USERS, D)
    value_blocks = event_values.reshape(N_SEQ, BLOCK_ROWS, USERS, D)
    user_ids = jnp.arange(USERS, dtype=jnp.int32)[:, None]

    def span_step(totals, span_index):
        key_total, value_total = totals
        first_row = span_index * SPAN_ROWS
        query_span = lax.dynamic_slice_in_dim(queries, first_row, SPAN_ROWS, 0)
        gate_value = lax.dynamic_slice_in_dim(gate_pre, first_row, SPAN_ROWS, 0).astype(jnp.float32)
        grad_out = lax.dynamic_slice_in_dim(out_grad, first_row, SPAN_ROWS, 0).astype(jnp.float32)
        gate_value = gate_value.reshape(SPAN_ROWS, USERS, HEADS, HEAD_DIM)
        grad_out = grad_out.reshape(SPAN_ROWS, USERS, HEADS, HEAD_DIM)
        offsets = lax.dynamic_index_in_dim(block_lists, span_index, 0, keepdims=False)
        blocks = ((span_index - offsets) % N_SEQ).astype(jnp.int32)
        usable = (blocks < history_len[:, None]).astype(jnp.float32)
        clipped = blocks
        key_heads = key_blocks[clipped, :, user_ids].astype(jnp.float32).reshape(USERS, ENTRIES * BLOCK_ROWS, HEADS, HEAD_DIM)
        value_heads = value_blocks[clipped, :, user_ids].astype(jnp.float32).reshape(USERS, ENTRIES * BLOCK_ROWS, HEADS, HEAD_DIM)
        key_mask = jnp.repeat(usable, BLOCK_ROWS, axis=1)[:, None, None, :]
        query_heads = query_span.astype(jnp.float32).reshape(SPAN_ROWS, USERS, HEADS, HEAD_DIM)
        scores = jnp.einsum('cuhd,ujhd->uhcj', query_heads, key_heads) * factor
        weights = (jax.nn.silu(scores) * key_mask).astype(jnp.bfloat16)
        attended = jnp.einsum('uhcj,ujhd->cuhd', weights.astype(jnp.float32), value_heads)
        inverse_root = lax.rsqrt(lax.optimization_barrier(jnp.mean(attended * attended, axis=-1, keepdims=True)) + EPS)
        normed = attended * inverse_root
        gate_silu = jax.nn.silu(gate_value)
        layer_out = (normed * gate_silu).astype(jnp.bfloat16)
        grad_gate = (grad_out * normed * silu_slope(gate_value)).astype(jnp.bfloat16)
        grad_normed = grad_out * gate_silu
        grad_attended = (inverse_root * (grad_normed - normed * lax.optimization_barrier(jnp.mean(grad_normed * normed, axis=-1, keepdims=True)))).astype(jnp.bfloat16)
        grad_heads = grad_attended.astype(jnp.float32)
        grad_weight = jnp.einsum('cuhd,ujhd->uhcj', grad_heads, value_heads)
        grad_scores = (grad_weight * silu_slope(scores) * factor * key_mask).astype(jnp.bfloat16)
        grad_query = jnp.einsum('uhcj,ujhd->cuhd', grad_scores.astype(jnp.float32), key_heads)
        key_part = jnp.einsum('uhcj,cuhd->ujhd', grad_scores.astype(jnp.float32), query_heads).reshape(USERS, ENTRIES, BLOCK_ROWS, D)
        value_part = jnp.einsum('uhcj,cuhd->ujhd', weights.astype(jnp.float32), grad_heads).reshape(USERS, ENTRIES, BLOCK_ROWS, D)
        key_total = key_total.at[clipped, :, user_ids].add(key_part)
        value_total = value_total.at[clipped, :, user_ids].add(value_part)
        shaped = (SPAN_ROWS, USERS, D)
        return ((key_total, value_total), (layer_out.reshape(shaped), grad_query.reshape(shaped).astype(jnp.bfloat16), grad_gate.reshape(shaped)))
    zero_total = jnp.zeros((N_SEQ, BLOCK_ROWS, USERS, D), jnp.float32)
    (key_total, value_total), stacked = lax.scan(span_step, (zero_total, zero_total), jnp.arange(N_SEQ, dtype=jnp.int32))
    layer_out = stacked[0].reshape(LATENTS, USERS, D)
    grad_queries = stacked[1].reshape(LATENTS, USERS, D)
    grad_gate = stacked[2].reshape(LATENTS, USERS, D)
    grad_keys = key_total.reshape(EVENTS, USERS, D).astype(jnp.bfloat16)
    grad_values = value_total.reshape(EVENTS, USERS, D).astype(jnp.bfloat16)
    return (layer_out, grad_queries, grad_gate, grad_keys, grad_values)
```

```python
import functools

import jax
import jax.numpy as jnp
from jax import lax
from jax.experimental import pallas as pl
from jax.experimental.pallas import tpu as pltpu
from jax.sharding import PartitionSpec as P

HEAD_DIM = 64
EPS = 1e-06
SLOTS = 2
PAIR = 2 * HEAD_DIM
TILE = 256
GROUP = 64
MERGE = 128
F32 = jnp.float32
BF16 = jnp.bfloat16
NT = (((1,), (1,)), ((), ()))
NN = (((1,), (0,)), ((), ()))
MESH = pl.DeviceIdType.MESH


def dot(a, b, dims):
    return lax.dot_general(a, b, dims, preferred_element_type=F32)


def split_heads(rows):
    lane = lax.broadcasted_iota(jnp.int32, rows.shape, 1)
    zero = jnp.zeros_like(rows)
    return jnp.concatenate(
        [jnp.where(lane < HEAD_DIM, rows, zero), jnp.where(lane < HEAD_DIM, zero, rows)], axis=0
    )


def join_heads(flipped):
    half = flipped.shape[1] // 2
    return jnp.concatenate([flipped[:HEAD_DIM, :half], flipped[HEAD_DIM:, half:]], axis=0).T


def lanes(f):
    return slice(f * PAIR, (f + 1) * PAIR)


def kernel(n, chunks, lists, lens, queries, gates, grads, keys, values,
           small_out, dkeys, dvalues,
           raw, small, k_buf, v_buf, t_buf, w_buf, s_buf, q_dense, d_dense, a_dense, d_own, stage,
           sends_q, recvs_q, sends, recvs,
           user_hold, slot_hold, user_own, slot_own,
           send_sem, first_sem, recv_sem, load_sem, store_sem):
    users, events = k_buf.shape[1:3]
    rows = queries.shape[0]
    latents = n * rows
    pieces = 2 * latents // PAIR
    me = lax.axis_index("seq")

    def load_copy(i, f):
        return pltpu.make_async_copy(
            (keys, values)[i].at[:, :, lanes(f)], raw.at[i, f % 2], load_sem.at[i, f])

    for f in range(min(2, chunks)):
        load_copy(0, f).start()
        load_copy(1, f).start()

    barrier = pltpu.get_barrier_semaphore()

    def greet(d, carry):
        pl.semaphore_signal(barrier, inc=1, device_id={"seq": lax.rem(me + d, n)},
                            device_id_type=MESH)
        return carry

    lax.fori_loop(1, n, greet, 0)

    def tables(own, p, carry):
        for user_of, slot_of, span, block in (
            ((user_own, slot_own, me, p),) if own else ((user_hold, slot_hold, p, me),)
        ):
            offset = lax.rem(span - block + n, n)
            count = jnp.int32(0)
            named = [jnp.int32(0)] * SLOTS
            for u in range(users):
                hit = lists[u, 0, span] == offset
                for i in range(1, lists.shape[1]):
                    hit = hit | (lists[u, i, span] == offset)
                hit = hit & (block < lens[u])
                slot_of[p, u] = jnp.where(hit, count, SLOTS)
                for s in range(SLOTS):
                    named[s] = jnp.where(hit & (count == s), u, named[s])
                count = count + jnp.where(hit, 1, 0)
            for s in range(SLOTS):
                user_of[p, s] = named[s]
        return carry

    lax.fori_loop(0, n, functools.partial(tables, True), 0)
    for i, (source, scale) in enumerate(((queries, 0.0625), (gates, None), (grads, None))):
        whole = jnp.swapaxes(source[...], 0, 1)
        if scale is not None:
            whole = (whole * scale).astype(BF16)
        for f in range(chunks):
            small[i, f] = whole[:, :, lanes(f)]

    for p in range(n):
        stage[p, SLOTS] = jnp.zeros((rows, PAIR), BF16)

    def copy_q(to, slot):
        return pltpu.make_async_remote_copy(
            src_ref=sends_q.at[to], dst_ref=recvs_q.at[slot],
            send_sem=send_sem.at[0], recv_sem=first_sem.at[0],
            device_id={"seq": to}, device_id_type=MESH)

    def exchange_q():
        def own(f, carry):
            for s in range(SLOTS):
                recvs_q[me, f, s] = small[0, f, user_own[me, s]]
            return carry

        lax.fori_loop(0, chunks, own, 0)

        def step(d, carry):
            to = lax.rem(me + d, n)
            for f in range(chunks):
                for s in range(SLOTS):
                    sends_q[to, f, s] = small[0, f, user_own[to, s]]
            copy_q(to, me).start()
            return carry

        lax.fori_loop(1, n, step, 0)

    def arrive_q():
        every = pl.ds(0, n - 1)
        pltpu.make_async_remote_copy(
            src_ref=sends_q.at[every], dst_ref=recvs_q.at[every],
            send_sem=send_sem.at[0], recv_sem=first_sem.at[0],
            device_id={"seq": lax.rem(me + 1, n)}, device_id_type=MESH).wait_recv()

    def copy(ph, f, to, slot):
        return pltpu.make_async_remote_copy(
            src_ref=sends.at[ph - 1, f, to], dst_ref=recvs.at[ph - 1, f, slot],
            send_sem=send_sem.at[ph], recv_sem=recv_sem.at[ph - 1, f],
            device_id={"seq": to}, device_id_type=MESH)

    def exchange(ph, f, read, user_of):
        for s in range(SLOTS):
            recvs[ph - 1, f, me, s] = read(user_of[me, s], me)

        def step(d, carry):
            to = lax.rem(me + d, n)
            for s in range(SLOTS):
                sends[ph - 1, f, to, s] = read(user_of[to, s], to)
            copy(ph, f, to, me).start()
            return carry

        lax.fori_loop(1, n, step, 0)

    def arrive(ph, f):
        every = pl.ds(0, n - 1)
        pltpu.make_async_remote_copy(
            src_ref=sends.at[ph - 1, f, every], dst_ref=recvs.at[ph - 1, f, every],
            send_sem=send_sem.at[ph], recv_sem=recv_sem.at[ph - 1, f],
            device_id={"seq": lax.rem(me + 1, n)}, device_id_type=MESH).wait_recv()

    def sent(ph):
        every = pl.ds(0, n - 1)
        ref = sends_q.at[every] if ph == 0 else sends.at[ph - 1, :, every]
        pltpu.make_async_remote_copy(
            src_ref=ref, dst_ref=ref, send_sem=send_sem.at[ph], recv_sem=first_sem.at[0],
            device_id={"seq": lax.rem(me + 1, n)}, device_id_type=MESH).wait_send()

    def spread(read, slot_of, dense):
        for p in range(n):
            for s in range(SLOTS):
                stage[p, s] = read(p, s)
        for u in range(users):
            for p in range(n):
                dense[u, p * rows:(p + 1) * rows] = stage[p, slot_of[p, u]]

    def gathered(ph, f, slot_of):
        for p in range(n):
            for s in range(SLOTS):
                stage[p, s] = recvs[ph - 1, f, p, s]
        out = []
        for u in range(users):
            total = stage[0, slot_of[0, u]].astype(F32)
            for p in range(1, n):
                total = total + stage[p, slot_of[p, u]].astype(F32)
            out.append(total)
        return jnp.concatenate(out, axis=0)

    def flip(buf, f):
        for u in range(users):
            for j in range(events // PAIR):
                t_buf[f, u, j] = buf[f, u, j * PAIR:(j + 1) * PAIR].T

    def flipped(f, u):
        return jnp.concatenate([t_buf[f, u, j] for j in range(events // PAIR)], axis=1)

    def wide(buf, f, u, tile):
        return jnp.concatenate([buf[f, u, h, tile] for h in range(pieces)], axis=1)

    def prepare(f):
        for i, buf in enumerate((k_buf, v_buf)):
            load_copy(i, f).wait()

            def split(g, carry):
                at = pl.ds(pl.multiple_of(g * GROUP, GROUP), GROUP)
                buf[f, :, at] = jnp.swapaxes(raw[i, f % 2, at], 0, 1)
                return carry

            with jax.named_scope("split"):
                lax.fori_loop(0, events // GROUP, split, 0)
            if f + 2 < chunks:
                load_copy(i, f + 2).start()

    def forward(f, carry):
        with jax.named_scope("flip_values"):
            flip(v_buf, f)
        with jax.named_scope("spread_queries"):
            spread(lambda p, s: recvs_q[p, f, s], slot_hold, q_dense.at[f])
        with jax.named_scope("attend"):
            for u in range(users):
                query = split_heads(q_dense[f, u])
                for j in range(0, events, TILE):
                    half = dot(k_buf[f, u, j:j + TILE], query, NT).astype(BF16)
                    bent = jnp.tanh(half)
                    up = 1.0 + bent
                    weight = half * up
                    slope = up + weight * (1.0 - bent)
                    for h in range(pieces):
                        w_buf[f, u, h, j:j + TILE] = weight[:, lanes(h)]
                        s_buf[f, u, h, j:j + TILE] = slope[:, lanes(h)]
                a_dense[f, u] = join_heads(
                    dot(flipped(f, u), wide(w_buf, f, u, slice(None)), NN).astype(BF16)
                ).reshape(n, rows, PAIR)
        with jax.named_scope("send_attended"):
            exchange(1, f, lambda u, c: a_dense[f, u, c], user_hold)
        return carry

    lane_a = lax.broadcasted_iota(jnp.int32, (PAIR, PAIR), 0) // HEAD_DIM
    lane_b = lax.broadcasted_iota(jnp.int32, (PAIR, PAIR), 1) // HEAD_DIM

    def middle(f, carry):
        averager = jnp.where(lane_a == lane_b, 1.0 / HEAD_DIM, 0.0).astype(F32)

        def head_mean(x):
            return lax.dot_general(x, averager, NN, preferred_element_type=F32,
                                   precision=lax.Precision.HIGHEST)

        with jax.named_scope("wait_attended"):
            arrive(1, f)
        with jax.named_scope("middle"):
            attended = gathered(1, f, slot_own)
            gate = small[1, f].reshape(users * rows, PAIR).astype(F32)
            grad = small[2, f].reshape(users * rows, PAIR).astype(F32)
            root = lax.rsqrt(head_mean(attended * attended) + EPS)
            normed = attended * root
            logistic = jax.nn.sigmoid(gate)
            gate_silu = gate * logistic
            slope = logistic * (1.0 + gate * (1.0 - logistic))
            shape = (users, rows, PAIR)
            small_out[0, f] = (normed * gate_silu).astype(BF16).reshape(shape)
            small_out[2, f] = (grad * normed * slope).astype(BF16).reshape(shape)
            grad_normed = grad * gate_silu
            back = root * (grad_normed - normed * head_mean(grad_normed * normed))
            d_own[f] = back.astype(BF16).reshape(shape)
            exchange(2, f, lambda u, c: d_own[f, u], user_own)
        with jax.named_scope("flip_keys"):
            flip(k_buf, f)
        return carry

    def backward(f, carry):
        with jax.named_scope("wait_grads"):
            arrive(2, f)
        with jax.named_scope("spread_grads"):
            spread(lambda p, s: recvs[1, f, p, s], slot_hold, d_dense.at[f])
        with jax.named_scope("query_grads"):
            for u in range(users):
                grad = split_heads(d_dense[f, u])
                for j in range(0, events, TILE):
                    grad_weight = dot(v_buf[f, u, j:j + TILE], grad, NT).astype(BF16)
                    for h in range(pieces):
                        s_buf[f, u, h, j:j + TILE] = (
                            grad_weight[:, lanes(h)] * s_buf[f, u, h, j:j + TILE])
                a_dense[f, u] = join_heads(
                    (dot(flipped(f, u), wide(s_buf, f, u, slice(None)), NN) * 0.0625).astype(BF16)
                ).reshape(n, rows, PAIR)
        with jax.named_scope("send_query_grads"):
            exchange(3, f, lambda u, c: a_dense[f, u, c], user_hold)
        return carry

    def store_copy(i, f):
        return pltpu.make_async_copy(
            (k_buf, v_buf)[i].at[f], (dkeys, dvalues)[i].at[f], store_sem.at[i])

    def event_grads(f, carry):
        with jax.named_scope("event_grads"):
            for u in range(users):
                query = split_heads(q_dense[f, u])
                grad = split_heads(d_dense[f, u])
                for j in range(0, events, TILE):
                    tile = slice(j, j + TILE)
                    v_buf[f, u, tile] = dot(wide(w_buf, f, u, tile), grad, NN).astype(BF16)
                    k_buf[f, u, tile] = dot(wide(s_buf, f, u, tile), query, NN).astype(BF16)
            store_copy(0, f).start()
            store_copy(1, f).start()
        return carry

    def finish(f, carry):
        with jax.named_scope("wait_query_grads"):
            arrive(3, f)
        with jax.named_scope("finish"):
            small_out[1, f] = gathered(3, f, slot_own).astype(BF16).reshape(users, rows, PAIR)
        return carry

    prepare(0)
    with jax.named_scope("barrier"):
        pl.semaphore_wait(barrier, n - 1)
    with jax.named_scope("send_queries"):
        exchange_q()
    lax.fori_loop(0, n, functools.partial(tables, False), 0)
    for f in range(1, chunks):
        prepare(f)
    with jax.named_scope("wait_queries"):
        arrive_q()
    lax.fori_loop(0, chunks, forward, 0)
    lax.fori_loop(0, chunks, middle, 0)
    lax.fori_loop(0, chunks, backward, 0)
    lax.fori_loop(0, chunks, event_grads, 0)
    lax.fori_loop(0, chunks, finish, 0)
    with jax.named_scope("drain"):
        for ph in range(4):
            sent(ph)
        for i, (buf, out) in enumerate(((k_buf, dkeys), (v_buf, dvalues))):
            pltpu.make_async_copy(buf, out, store_sem.at[i]).wait()


def lay_out(small_in, dkeys, dvalues, layer_out, grad_queries, grad_gate, out_keys, out_values):
    chunks = small_in.shape[1]
    block = out_keys.shape[0]

    @pl.when(pl.program_id(0) == 0)
    def _():
        for i, out in enumerate((layer_out, grad_queries, grad_gate)):
            for f in range(chunks):
                out[:, :, lanes(f)] = jnp.swapaxes(small_in[i, f], 0, 1)

    for source, out in ((dkeys, out_keys), (dvalues, out_values)):
        for f in range(chunks):
            for g in range(0, block, GROUP):
                out[g:g + GROUP, :, lanes(f)] = jnp.swapaxes(source[f, :, g:g + GROUP], 0, 1)


def body(n, queries, gate_pre, event_keys, event_values, block_lists, history_len, out_grad):
    rows, users, width = queries.shape
    events = event_keys.shape[0]
    chunks = width // PAIR
    latents = n * rows
    vmem = pl.BlockSpec(memory_space=pltpu.VMEM)
    smem = pl.BlockSpec(memory_space=pltpu.SMEM)
    hbm = pl.BlockSpec(memory_space=pl.ANY)
    table = [pltpu.SMEM((n, SLOTS), jnp.int32), pltpu.SMEM((n, users), jnp.int32)]
    flops = 6 * 2 * users * width * latents * events
    packed = (chunks, users, events, PAIR)
    small_out, dkeys, dvalues = pl.pallas_call(
        functools.partial(kernel, n, chunks),
        out_shape=(
            jax.ShapeDtypeStruct((3, chunks, users, rows, PAIR), BF16),
            jax.ShapeDtypeStruct(packed, BF16),
            jax.ShapeDtypeStruct(packed, BF16),
        ),
        in_specs=[smem, smem, vmem, vmem, vmem, hbm, hbm],
        out_specs=(vmem, hbm, hbm),
        scratch_shapes=[
            pltpu.VMEM((2, 2, events, users, PAIR), BF16),
            pltpu.VMEM((3, chunks, users, rows, PAIR), BF16),
            pltpu.VMEM(packed, BF16),
            pltpu.VMEM(packed, BF16),
            pltpu.VMEM((chunks, users, events // PAIR, PAIR, PAIR), BF16),
            pltpu.VMEM((chunks, users, 2 * latents // PAIR, events, PAIR), BF16),
            pltpu.VMEM((chunks, users, 2 * latents // PAIR, events, PAIR), BF16),
            pltpu.VMEM((chunks, users, latents, PAIR), BF16),
            pltpu.VMEM((chunks, users, latents, PAIR), BF16),
            pltpu.VMEM((chunks, users, n, rows, PAIR), BF16),
            pltpu.VMEM((chunks, users, rows, PAIR), BF16),
            pltpu.VMEM((n, SLOTS + 1, rows, PAIR), BF16),
            pltpu.VMEM((n, chunks, SLOTS, rows, PAIR), BF16),
            pltpu.VMEM((n, chunks, SLOTS, rows, PAIR), BF16),
            pltpu.VMEM((3, chunks, n, SLOTS, rows, PAIR), BF16),
            pltpu.VMEM((3, chunks, n, SLOTS, rows, PAIR), BF16),
            *table,
            *table,
            pltpu.SemaphoreType.DMA((4,)),
            pltpu.SemaphoreType.DMA((1,)),
            pltpu.SemaphoreType.DMA((3, chunks)),
            pltpu.SemaphoreType.DMA((2, chunks)),
            pltpu.SemaphoreType.DMA((2,)),
        ],
        compiler_params=pltpu.CompilerParams(
            collective_id=0, has_side_effects=True, vmem_limit_bytes=62 * 1024 * 1024
        ),
        cost_estimate=pl.CostEstimate(
            flops=flops, bytes_accessed=8 * users * events * width, transcendentals=0),
        name="sparse_attention",
    )(block_lists.transpose(1, 2, 0), history_len, queries, gate_pre, out_grad,
      event_keys, event_values)

    tiny = jax.ShapeDtypeStruct((rows, users, width), BF16)
    large = jax.ShapeDtypeStruct((events, users, width), BF16)
    tiny_spec = pl.BlockSpec((rows, users, width), lambda i: (0, 0, 0))
    large_spec = pl.BlockSpec((MERGE, users, width), lambda i: (i, 0, 0))
    part = pl.BlockSpec((chunks, users, MERGE, PAIR), lambda i: (0, 0, i, 0))
    return pl.pallas_call(
        lay_out,
        grid=(events // MERGE,),
        out_shape=(tiny, tiny, tiny, large, large),
        in_specs=[
            pl.BlockSpec((3, chunks, users, rows, PAIR), lambda i: (0, 0, 0, 0, 0)), part, part],
        out_specs=(tiny_spec, tiny_spec, tiny_spec, large_spec, large_spec),
        compiler_params=pltpu.CompilerParams(vmem_limit_bytes=32 * 1024 * 1024),
        cost_estimate=pl.CostEstimate(
            flops=0, bytes_accessed=8 * users * events * width, transcendentals=0),
        name="lay_out",
    )(small_out, dkeys, dvalues)


def solution(mesh):
    shard = P("seq", "dp", "head")
    return jax.shard_map(
        functools.partial(body, mesh.shape["seq"]),
        mesh=mesh,
        in_specs=(shard, shard, shard, shard, P(None, "dp", None), P("dp"), shard),
        out_specs=(shard,) * 5,
        check_vma=False,
    )
```

```python
import functools

import jax
import jax.numpy as jnp
from jax import lax
from jax.experimental import pallas as pl
from jax.experimental.pallas import tpu as pltpu
from jax.sharding import PartitionSpec as P

HEAD_DIM = 64
EPS = 1e-06
SLOTS = 2
PAIR = 2 * HEAD_DIM
TILE = 256
SPLIT = 256
MERGE = 128
F32 = jnp.float32
BF16 = jnp.bfloat16
NT = (((1,), (1,)), ((), ()))
NN = (((1,), (0,)), ((), ()))
MESH = pl.DeviceIdType.MESH


def dot(a, b, dims):
    return lax.dot_general(a, b, dims, preferred_element_type=F32)


def split_heads(rows):
    lane = lax.broadcasted_iota(jnp.int32, rows.shape, 1)
    zero = jnp.zeros_like(rows)
    return jnp.concatenate(
        [jnp.where(lane < HEAD_DIM, rows, zero), jnp.where(lane < HEAD_DIM, zero, rows)], axis=0
    )


def join_heads(flipped):
    half = flipped.shape[1] // 2
    return jnp.concatenate([flipped[:HEAD_DIM, :half], flipped[HEAD_DIM:, half:]], axis=0).T


def lanes(f):
    return slice(f * PAIR, (f + 1) * PAIR)


def kernel(n, chunks, lists, lens, queries, gates, grads, keys, values,
           small_out, dkeys, dvalues,
           raw, mixed, small, k_buf, v_buf, w_buf, s_buf, q_dense, d_dense, a_dense, d_own, stage,
           sends, recvs,
           user_hold, slot_hold, user_own, slot_own,
           send_sem, recv_sem, load_sem, store_sem):
    users, events = k_buf.shape[1:3]
    rows = queries.shape[0]
    latents = n * rows
    pieces = 2 * latents // PAIR
    me = lax.axis_index("seq")

    def load_copy(i, f):
        return pltpu.make_async_copy(
            (keys, values)[i].at[:, :, lanes(f)], raw.at[i, f % 2], load_sem.at[i, f])

    for f in range(min(2, chunks)):
        load_copy(0, f).start()
        load_copy(1, f).start()

    barrier = pltpu.get_barrier_semaphore()

    def greet(d, carry):
        pl.semaphore_signal(barrier, inc=1, device_id={"seq": lax.rem(me + d, n)},
                            device_id_type=MESH)
        return carry

    lax.fori_loop(1, n, greet, 0)

    def tables(own, p, carry):
        for user_of, slot_of, span, block in (
            ((user_own, slot_own, me, p),) if own else ((user_hold, slot_hold, p, me),)
        ):
            offset = lax.rem(span - block + n, n)
            count = jnp.int32(0)
            named = [jnp.int32(0)] * SLOTS
            for u in range(users):
                hit = lists[u, 0, span] == offset
                for i in range(1, lists.shape[1]):
                    hit = hit | (lists[u, i, span] == offset)
                hit = hit & (block < lens[u])
                slot_of[p, u] = jnp.where(hit, count, SLOTS)
                for s in range(SLOTS):
                    named[s] = jnp.where(hit & (count == s), u, named[s])
                count = count + jnp.where(hit, 1, 0)
            for s in range(SLOTS):
                user_of[p, s] = named[s]
        return carry

    lax.fori_loop(0, n, functools.partial(tables, True), 0)
    def sort_users(i, whole):
        for f in range(chunks):
            small[i, f] = jnp.swapaxes(whole[:, :, lanes(f)], 0, 1)

    sort_users(0, (queries[...] * 0.0625).astype(BF16))

    def copy(ph, f, to, slot):
        return pltpu.make_async_remote_copy(
            src_ref=sends.at[ph, f, to], dst_ref=recvs.at[ph, f, slot],
            send_sem=send_sem.at[ph], recv_sem=recv_sem.at[ph, f],
            device_id={"seq": to}, device_id_type=MESH)

    def exchange(ph, f, read, user_of):
        for s in range(SLOTS):
            recvs[ph, f, me, s] = read(user_of[me, s], me)

        def step(d, carry):
            to = lax.rem(me + d, n)
            for s in range(SLOTS):
                sends[ph, f, to, s] = read(user_of[to, s], to)
            copy(ph, f, to, me).start()
            return carry

        lax.fori_loop(1, n, step, 0)

    def arrive(ph, f):
        every = pl.ds(0, n - 1)
        pltpu.make_async_remote_copy(
            src_ref=sends.at[ph, f, every], dst_ref=recvs.at[ph, f, every],
            send_sem=send_sem.at[ph], recv_sem=recv_sem.at[ph, f],
            device_id={"seq": lax.rem(me + 1, n)}, device_id_type=MESH).wait_recv()

    def sent(ph):
        ref = sends.at[ph, :, pl.ds(0, n - 1)]
        pltpu.make_async_remote_copy(
            src_ref=ref, dst_ref=ref, send_sem=send_sem.at[ph], recv_sem=recv_sem.at[ph, 0],
            device_id={"seq": lax.rem(me + 1, n)}, device_id_type=MESH).wait_send()

    def spread(read, slot_of, dense):
        for p in range(n):
            for s in range(SLOTS):
                stage[p, s] = read(p, s)
        for u in range(users):
            for p in range(n):
                dense[u, p * rows:(p + 1) * rows] = stage[p, slot_of[p, u]]

    def gathered(ph, f, slot_of):
        for p in range(n):
            for s in range(SLOTS):
                stage[p, s] = recvs[ph, f, p, s]
        out = []
        for u in range(users):
            total = stage[0, slot_of[0, u]].astype(F32)
            for p in range(1, n):
                total = total + stage[p, slot_of[p, u]].astype(F32)
            out.append(total)
        return jnp.concatenate(out, axis=0)

    def flipped(buf, f, u):
        return jnp.concatenate(
            [buf[f, u, j:j + PAIR].T for j in range(0, events, PAIR)], axis=1)

    def wide(buf, f, u, tile):
        return jnp.concatenate([buf[f, u, h, tile] for h in range(pieces)], axis=1)

    def prepare(f):
        for i, buf in enumerate((k_buf, v_buf)):
            load_copy(i, f).wait()

            def split(g, carry):
                at = pl.ds(pl.multiple_of(g * SPLIT, SPLIT), SPLIT)
                mixed[...] = raw[i, f % 2, at].astype(F32).reshape(SPLIT * users, PAIR)
                for u in range(users):
                    buf[f, u, at] = mixed[pl.ds(u, SPLIT, users), :].astype(BF16)
                return carry

            with jax.named_scope("split"):
                lax.fori_loop(0, events // SPLIT, split, 0)
            if f + 2 < chunks:
                load_copy(i, f + 2).start()

    def forward(f, carry):
        with jax.named_scope("wait_queries"):
            arrive(0, f)
        with jax.named_scope("spread_queries"):
            spread(lambda p, s: recvs[0, f, p, s], slot_hold, q_dense.at[f])
        with jax.named_scope("attend"):
            for u in range(users):
                query = split_heads(q_dense[f, u])
                weights = []
                for j in range(0, events, TILE):
                    half = dot(k_buf[f, u, j:j + TILE], query, NT).astype(BF16)
                    bent = jnp.tanh(half)
                    up = 1.0 + bent
                    weight = half * up
                    slope = up + weight * (1.0 - bent)
                    weights.append(weight)
                    for h in range(pieces):
                        w_buf[f, u, h, j:j + TILE] = weight[:, lanes(h)]
                        s_buf[f, u, h, j:j + TILE] = slope[:, lanes(h)]
                a_dense[f, u] = join_heads(
                    dot(flipped(v_buf, f, u), jnp.concatenate(weights, axis=0), NN).astype(BF16)
                ).reshape(n, rows, PAIR)
        with jax.named_scope("send_attended"):
            exchange(1, f, lambda u, c: a_dense[f, u, c], user_hold)
        return carry

    lane_a = lax.broadcasted_iota(jnp.int32, (PAIR, PAIR), 0) // HEAD_DIM
    lane_b = lax.broadcasted_iota(jnp.int32, (PAIR, PAIR), 1) // HEAD_DIM

    def middle(f, carry):
        averager = jnp.where(lane_a == lane_b, 1.0 / HEAD_DIM, 0.0).astype(F32)

        def head_mean(x):
            return lax.dot_general(x, averager, NN, preferred_element_type=F32,
                                   precision=lax.Precision.HIGHEST)

        with jax.named_scope("wait_attended"):
            arrive(1, f)
        with jax.named_scope("middle"):
            attended = gathered(1, f, slot_own)
            gate = small[1, f].reshape(users * rows, PAIR).astype(F32)
            grad = small[2, f].reshape(users * rows, PAIR).astype(F32)
            root = lax.rsqrt(head_mean(attended * attended) + EPS)
            normed = attended * root
            logistic = jax.nn.sigmoid(gate)
            gate_silu = gate * logistic
            slope = logistic * (1.0 + gate * (1.0 - logistic))
            shape = (users, rows, PAIR)
            small_out[0, f] = (normed * gate_silu).astype(BF16).reshape(shape)
            small_out[2, f] = (grad * normed * slope).astype(BF16).reshape(shape)
            grad_normed = grad * gate_silu
            back = root * (grad_normed - normed * head_mean(grad_normed * normed))
            d_own[f] = back.astype(BF16).reshape(shape)
            exchange(2, f, lambda u, c: d_own[f, u], user_own)
        return carry

    def backward(f, carry):
        with jax.named_scope("wait_grads"):
            arrive(2, f)
        with jax.named_scope("spread_grads"):
            spread(lambda p, s: recvs[2, f, p, s], slot_hold, d_dense.at[f])
        with jax.named_scope("query_grads"):
            for u in range(users):
                grad = split_heads(d_dense[f, u])
                grad_scores = []
                for j in range(0, events, TILE):
                    grad_weight = dot(v_buf[f, u, j:j + TILE], grad, NT).astype(BF16)
                    grad_score = grad_weight * wide(s_buf, f, u, slice(j, j + TILE))
                    grad_scores.append(grad_score)
                    for h in range(pieces):
                        s_buf[f, u, h, j:j + TILE] = grad_score[:, lanes(h)]
                a_dense[f, u] = join_heads(
                    (dot(flipped(k_buf, f, u), jnp.concatenate(grad_scores, axis=0), NN)
                     * 0.0625).astype(BF16)
                ).reshape(n, rows, PAIR)
        with jax.named_scope("send_query_grads"):
            exchange(3, f, lambda u, c: a_dense[f, u, c], user_hold)
        return carry

    def store_copy(i, f):
        return pltpu.make_async_copy(
            (k_buf, v_buf)[i].at[f], (dkeys, dvalues)[i].at[f], store_sem.at[i])

    def event_grads(f, carry):
        with jax.named_scope("event_grads"):
            for u in range(users):
                query = split_heads(q_dense[f, u])
                grad = split_heads(d_dense[f, u])
                for j in range(0, events, TILE):
                    tile = slice(j, j + TILE)
                    v_buf[f, u, tile] = dot(wide(w_buf, f, u, tile), grad, NN).astype(BF16)
                    k_buf[f, u, tile] = dot(wide(s_buf, f, u, tile), query, NN).astype(BF16)
            store_copy(0, f).start()
            store_copy(1, f).start()
        return carry

    def finish(f, carry):
        with jax.named_scope("wait_query_grads"):
            arrive(3, f)
        with jax.named_scope("finish"):
            small_out[1, f] = gathered(3, f, slot_own).astype(BF16).reshape(users, rows, PAIR)
        return carry

    with jax.named_scope("barrier"):
        pl.semaphore_wait(barrier, n - 1)
    with jax.named_scope("send_queries"):
        def send_queries(f, carry):
            exchange(0, f, lambda u, c: small[0, f, u], user_own)
            return carry

        lax.fori_loop(0, chunks, send_queries, 0)
    lax.fori_loop(0, n, functools.partial(tables, False), 0)
    sort_users(1, gates[...])
    sort_users(2, grads[...])
    for p in range(n):
        stage[p, SLOTS] = jnp.zeros((rows, PAIR), BF16)
    for f in range(chunks):
        prepare(f)

    ahead = min(2, chunks)

    def first(f, carry):
        forward(f, 0)

        @pl.when(f >= ahead)
        def _():
            middle(f - ahead, 0)

        return carry

    def second(f, carry):
        @pl.when(f < ahead)
        def _():
            middle(f + chunks - ahead, 0)

        return backward(f, carry)

    lax.fori_loop(0, chunks, first, 0)
    lax.fori_loop(0, chunks, second, 0)
    lax.fori_loop(0, chunks, event_grads, 0)
    lax.fori_loop(0, chunks, finish, 0)
    with jax.named_scope("drain"):
        for ph in range(4):
            sent(ph)
        for i, (buf, out) in enumerate(((k_buf, dkeys), (v_buf, dvalues))):
            pltpu.make_async_copy(buf, out, store_sem.at[i]).wait()


def lay_out(small_in, dkeys, dvalues, layer_out, grad_queries, grad_gate, out_keys, out_values):
    chunks, users = small_in.shape[1:3]
    block = out_keys.shape[0]

    @pl.when(pl.program_id(0) == 0)
    def _():
        for i, out in enumerate((layer_out, grad_queries, grad_gate)):
            for f in range(chunks):
                out[:, :, lanes(f)] = jnp.swapaxes(small_in[i, f], 0, 1)

    for source, out in ((dkeys, out_keys), (dvalues, out_values)):
        for f in range(chunks):
            joined = jnp.concatenate([source[f, u] for u in range(users)], axis=1)
            out[:, :, lanes(f)] = joined.reshape(block, users, PAIR)


def body(n, queries, gate_pre, event_keys, event_values, block_lists, history_len, out_grad):
    rows, users, width = queries.shape
    events = event_keys.shape[0]
    chunks = width // PAIR
    latents = n * rows
    vmem = pl.BlockSpec(memory_space=pltpu.VMEM)
    smem = pl.BlockSpec(memory_space=pltpu.SMEM)
    hbm = pl.BlockSpec(memory_space=pl.ANY)
    table = [pltpu.SMEM((n, SLOTS), jnp.int32), pltpu.SMEM((n, users), jnp.int32)]
    flops = 6 * 2 * users * width * latents * events
    packed = (chunks, users, events, PAIR)
    small_out, dkeys, dvalues = pl.pallas_call(
        functools.partial(kernel, n, chunks),
        out_shape=(
            jax.ShapeDtypeStruct((3, chunks, users, rows, PAIR), BF16),
            jax.ShapeDtypeStruct(packed, BF16),
            jax.ShapeDtypeStruct(packed, BF16),
        ),
        in_specs=[smem, smem, vmem, vmem, vmem, hbm, hbm],
        out_specs=(vmem, hbm, hbm),
        scratch_shapes=[
            pltpu.VMEM((2, 2, events, users, PAIR), BF16),
            pltpu.VMEM((SPLIT * users, PAIR), F32),
            pltpu.VMEM((3, chunks, users, rows, PAIR), BF16),
            pltpu.VMEM(packed, BF16),
            pltpu.VMEM(packed, BF16),
            pltpu.VMEM((chunks, users, 2 * latents // PAIR, events, PAIR), BF16),
            pltpu.VMEM((chunks, users, 2 * latents // PAIR, events, PAIR), BF16),
            pltpu.VMEM((chunks, users, latents, PAIR), BF16),
            pltpu.VMEM((chunks, users, latents, PAIR), BF16),
            pltpu.VMEM((chunks, users, n, rows, PAIR), BF16),
            pltpu.VMEM((chunks, users, rows, PAIR), BF16),
            pltpu.VMEM((n, SLOTS + 1, rows, PAIR), BF16),
            pltpu.VMEM((4, chunks, n, SLOTS, rows, PAIR), BF16),
            pltpu.VMEM((4, chunks, n, SLOTS, rows, PAIR), BF16),
            *table,
            *table,
            pltpu.SemaphoreType.DMA((4,)),
            pltpu.SemaphoreType.DMA((4, chunks)),
            pltpu.SemaphoreType.DMA((2, chunks)),
            pltpu.SemaphoreType.DMA((2,)),
        ],
        compiler_params=pltpu.CompilerParams(
            collective_id=0, has_side_effects=True, vmem_limit_bytes=62 * 1024 * 1024
        ),
        cost_estimate=pl.CostEstimate(
            flops=flops, bytes_accessed=8 * users * events * width, transcendentals=0),
        name="sparse_attention",
    )(block_lists.transpose(1, 2, 0), history_len, queries, gate_pre, out_grad,
      event_keys, event_values)

    tiny = jax.ShapeDtypeStruct((rows, users, width), BF16)
    large = jax.ShapeDtypeStruct((events, users, width), BF16)
    tiny_spec = pl.BlockSpec((rows, users, width), lambda i: (0, 0, 0))
    large_spec = pl.BlockSpec((MERGE, users, width), lambda i: (i, 0, 0))
    part = pl.BlockSpec((chunks, users, MERGE, PAIR), lambda i: (0, 0, i, 0))
    return pl.pallas_call(
        lay_out,
        grid=(events // MERGE,),
        out_shape=(tiny, tiny, tiny, large, large),
        in_specs=[
            pl.BlockSpec((3, chunks, users, rows, PAIR), lambda i: (0, 0, 0, 0, 0)), part, part],
        out_specs=(tiny_spec, tiny_spec, tiny_spec, large_spec, large_spec),
        compiler_params=pltpu.CompilerParams(vmem_limit_bytes=62 * 1024 * 1024),
        cost_estimate=pl.CostEstimate(
            flops=0, bytes_accessed=8 * users * events * width, transcendentals=0),
        name="lay_out",
    )(small_out, dkeys, dvalues)


def solution(mesh):
    shard = P("seq", "dp", "head")
    return jax.shard_map(
        functools.partial(body, mesh.shape["seq"]),
        mesh=mesh,
        in_specs=(shard, shard, shard, shard, P(None, "dp", None), P("dp"), shard),
        out_specs=(shard,) * 5,
        check_vma=False,
    )
```

```python
import functools

import jax
import jax.numpy as jnp
from jax import lax
from jax.experimental import pallas as pl
from jax.experimental.pallas import tpu as pltpu
from jax.sharding import PartitionSpec as P

HEAD_DIM = 64
EPS = 1e-06
SLOTS = 2
PAIR = 2 * HEAD_DIM
TILE = 256
SPLIT = 256
MERGE = 128
F32 = jnp.float32
BF16 = jnp.bfloat16
NT = (((1,), (1,)), ((), ()))
NN = (((1,), (0,)), ((), ()))
MESH = pl.DeviceIdType.MESH


def dot(a, b, dims):
    return lax.dot_general(a, b, dims, preferred_element_type=F32)


def split_heads(rows):
    lane = lax.broadcasted_iota(jnp.int32, rows.shape, 1)
    zero = jnp.zeros_like(rows)
    return jnp.concatenate(
        [jnp.where(lane < HEAD_DIM, rows, zero), jnp.where(lane < HEAD_DIM, zero, rows)], axis=0
    )


def join_heads(flipped):
    half = flipped.shape[1] // 2
    return jnp.concatenate([flipped[:HEAD_DIM, :half], flipped[HEAD_DIM:, half:]], axis=0).T


def lanes(f):
    return slice(f * PAIR, (f + 1) * PAIR)


def kernel(n, chunks, lists, lens, queries, gates, grads, keys, values,
           small_out, dkeys, dvalues,
           raw, mixed, small, k_buf, v_buf, w_buf, s_buf, q_dense, d_dense, a_dense, d_own, stage,
           sends, recvs,
           user_hold, slot_hold, user_own, slot_own,
           send_sem, recv_sem, load_sem):
    users, events = k_buf.shape[1:3]
    rows = queries.shape[0]
    latents = n * rows
    pieces = 2 * latents // PAIR
    me = lax.axis_index("seq")

    def load_copy(i, f):
        return pltpu.make_async_copy(
            (keys, values)[i].at[:, :, lanes(f)], raw.at[i, f % 2], load_sem.at[i, f])

    for f in range(min(2, chunks)):
        load_copy(0, f).start()
        load_copy(1, f).start()

    barrier = pltpu.get_barrier_semaphore()

    def greet(d, carry):
        pl.semaphore_signal(barrier, inc=1, device_id={"seq": lax.rem(me + d, n)},
                            device_id_type=MESH)
        return carry

    lax.fori_loop(1, n, greet, 0)

    def tables(own, p, carry):
        for user_of, slot_of, span, block in (
            ((user_own, slot_own, me, p),) if own else ((user_hold, slot_hold, p, me),)
        ):
            offset = lax.rem(span - block + n, n)
            count = jnp.int32(0)
            named = [jnp.int32(0)] * SLOTS
            for u in range(users):
                hit = lists[u, 0, span] == offset
                for i in range(1, lists.shape[1]):
                    hit = hit | (lists[u, i, span] == offset)
                hit = hit & (block < lens[u])
                slot_of[p, u] = jnp.where(hit, count, SLOTS)
                for s in range(SLOTS):
                    named[s] = jnp.where(hit & (count == s), u, named[s])
                count = count + jnp.where(hit, 1, 0)
            for s in range(SLOTS):
                user_of[p, s] = named[s]
        return carry

    lax.fori_loop(0, n, functools.partial(tables, True), 0)
    def sort_users(i, whole):
        for f in range(chunks):
            small[i, f] = jnp.swapaxes(whole[:, :, lanes(f)], 0, 1)

    sort_users(0, (queries[...] * 0.0625).astype(BF16))

    def copy(ph, f, to, slot):
        return pltpu.make_async_remote_copy(
            src_ref=sends.at[ph, f, to], dst_ref=recvs.at[ph, f, slot],
            send_sem=send_sem.at[ph], recv_sem=recv_sem.at[ph, f],
            device_id={"seq": to}, device_id_type=MESH)

    def exchange(ph, f, read, user_of):
        for s in range(SLOTS):
            recvs[ph, f, me, s] = read(user_of[me, s], me)

        def step(d, carry):
            to = lax.rem(me + d, n)
            for s in range(SLOTS):
                sends[ph, f, to, s] = read(user_of[to, s], to)
            copy(ph, f, to, me).start()
            return carry

        lax.fori_loop(1, n, step, 0)

    def arrive(ph, f):
        every = pl.ds(0, n - 1)
        pltpu.make_async_remote_copy(
            src_ref=sends.at[ph, f, every], dst_ref=recvs.at[ph, f, every],
            send_sem=send_sem.at[ph], recv_sem=recv_sem.at[ph, f],
            device_id={"seq": lax.rem(me + 1, n)}, device_id_type=MESH).wait_recv()

    def sent(ph):
        ref = sends.at[ph, :, pl.ds(0, n - 1)]
        pltpu.make_async_remote_copy(
            src_ref=ref, dst_ref=ref, send_sem=send_sem.at[ph], recv_sem=recv_sem.at[ph, 0],
            device_id={"seq": lax.rem(me + 1, n)}, device_id_type=MESH).wait_send()

    def spread(read, slot_of, dense):
        for p in range(n):
            for s in range(SLOTS):
                stage[p, s] = read(p, s)
        for u in range(users):
            for p in range(n):
                dense[u, p * rows:(p + 1) * rows] = stage[p, slot_of[p, u]]

    def gathered(ph, f, slot_of):
        for p in range(n):
            for s in range(SLOTS):
                stage[p, s] = recvs[ph, f, p, s]
        out = []
        for u in range(users):
            total = stage[0, slot_of[0, u]].astype(F32)
            for p in range(1, n):
                total = total + stage[p, slot_of[p, u]].astype(F32)
            out.append(total)
        return jnp.concatenate(out, axis=0)

    def flipped(buf, f, u):
        return jnp.concatenate(
            [buf[f, u, j:j + PAIR].T for j in range(0, events, PAIR)], axis=1)

    def wide(buf, f, u, tile):
        return jnp.concatenate([buf[f, u, h, tile] for h in range(pieces)], axis=1)

    def prepare(f):
        for i, buf in enumerate((k_buf, v_buf)):
            load_copy(i, f).wait()

            def split(g, carry):
                at = pl.ds(pl.multiple_of(g * SPLIT, SPLIT), SPLIT)
                mixed[...] = raw[i, f % 2, at].astype(F32).reshape(SPLIT * users, PAIR)
                for u in range(users):
                    buf[f, u, at] = mixed[pl.ds(u, SPLIT, users), :].astype(BF16)
                return carry

            with jax.named_scope("split"):
                lax.fori_loop(0, events // SPLIT, split, 0)
            if f + 2 < chunks:
                load_copy(i, f + 2).start()

    def forward(f, carry):
        with jax.named_scope("wait_queries"):
            arrive(0, f)
        with jax.named_scope("spread_queries"):
            spread(lambda p, s: recvs[0, f, p, s], slot_hold, q_dense.at[f])
        with jax.named_scope("attend"):
            for u in range(users):
                query = split_heads(q_dense[f, u])
                weights = []
                for j in range(0, events, TILE):
                    half = dot(k_buf[f, u, j:j + TILE], query, NT).astype(BF16)
                    bent = jnp.tanh(half)
                    up = 1.0 + bent
                    weight = half * up
                    slope = up + weight * (1.0 - bent)
                    weights.append(weight)
                    for h in range(pieces):
                        w_buf[f, u, h, j:j + TILE] = weight[:, lanes(h)]
                        s_buf[f, u, h, j:j + TILE] = slope[:, lanes(h)]
                a_dense[f, u] = join_heads(
                    dot(flipped(v_buf, f, u), jnp.concatenate(weights, axis=0), NN).astype(BF16)
                ).reshape(n, rows, PAIR)
        with jax.named_scope("send_attended"):
            exchange(1, f, lambda u, c: a_dense[f, u, c], user_hold)
        return carry

    lane_a = lax.broadcasted_iota(jnp.int32, (PAIR, PAIR), 0) // HEAD_DIM
    lane_b = lax.broadcasted_iota(jnp.int32, (PAIR, PAIR), 1) // HEAD_DIM

    def middle(f, carry):
        averager = jnp.where(lane_a == lane_b, 1.0 / HEAD_DIM, 0.0).astype(F32)

        def head_mean(x):
            return lax.dot_general(x, averager, NN, preferred_element_type=F32,
                                   precision=lax.Precision.HIGHEST)

        with jax.named_scope("wait_attended"):
            arrive(1, f)
        with jax.named_scope("middle"):
            attended = gathered(1, f, slot_own)
            gate = small[1, f].reshape(users * rows, PAIR).astype(F32)
            grad = small[2, f].reshape(users * rows, PAIR).astype(F32)
            root = lax.rsqrt(head_mean(attended * attended) + EPS)
            normed = attended * root
            logistic = jax.nn.sigmoid(gate)
            gate_silu = gate * logistic
            slope = logistic * (1.0 + gate * (1.0 - logistic))
            shape = (users, rows, PAIR)
            small_out[0, f] = (normed * gate_silu).astype(BF16).reshape(shape)
            small_out[2, f] = (grad * normed * slope).astype(BF16).reshape(shape)
            grad_normed = grad * gate_silu
            back = root * (grad_normed - normed * head_mean(grad_normed * normed))
            d_own[f] = back.astype(BF16).reshape(shape)
            exchange(2, f, lambda u, c: d_own[f, u], user_own)
        return carry

    def backward(f, carry):
        with jax.named_scope("wait_grads"):
            arrive(2, f)
        with jax.named_scope("spread_grads"):
            spread(lambda p, s: recvs[2, f, p, s], slot_hold, d_dense.at[f])
        with jax.named_scope("query_grads"):
            for u in range(users):
                grad = split_heads(d_dense[f, u])
                grad_scores = []
                for j in range(0, events, TILE):
                    grad_weight = dot(v_buf[f, u, j:j + TILE], grad, NT).astype(BF16)
                    grad_score = grad_weight * wide(s_buf, f, u, slice(j, j + TILE))
                    grad_scores.append(grad_score)
                    for h in range(pieces):
                        s_buf[f, u, h, j:j + TILE] = grad_score[:, lanes(h)]
                a_dense[f, u] = join_heads(
                    (dot(flipped(k_buf, f, u), jnp.concatenate(grad_scores, axis=0), NN)
                     * 0.0625).astype(BF16)
                ).reshape(n, rows, PAIR)
        with jax.named_scope("send_query_grads"):
            exchange(3, f, lambda u, c: a_dense[f, u, c], user_hold)
        return carry

    def event_grads(f, carry):
        with jax.named_scope("event_grads"):
            for u in range(users):
                query = split_heads(q_dense[f, u])
                grad = split_heads(d_dense[f, u])
                for j in range(0, events, TILE):
                    tile = slice(j, j + TILE)
                    dvalues[f, u, tile] = dot(wide(w_buf, f, u, tile), grad, NN).astype(BF16)
                    dkeys[f, u, tile] = dot(wide(s_buf, f, u, tile), query, NN).astype(BF16)
        return carry

    def finish(f, carry):
        with jax.named_scope("wait_query_grads"):
            arrive(3, f)
        with jax.named_scope("finish"):
            small_out[1, f] = gathered(3, f, slot_own).astype(BF16).reshape(users, rows, PAIR)
        return carry

    with jax.named_scope("barrier"):
        pl.semaphore_wait(barrier, n - 1)
    with jax.named_scope("send_queries"):
        def send_queries(f, carry):
            exchange(0, f, lambda u, c: small[0, f, u], user_own)
            return carry

        lax.fori_loop(0, chunks, send_queries, 0)
    lax.fori_loop(0, n, functools.partial(tables, False), 0)
    sort_users(1, gates[...])
    sort_users(2, grads[...])
    for p in range(n):
        stage[p, SLOTS] = jnp.zeros((rows, PAIR), BF16)
    for f in range(chunks):
        prepare(f)

    ahead = min(2, chunks)

    def first(f, carry):
        forward(f, 0)

        @pl.when(f >= ahead)
        def _():
            middle(f - ahead, 0)

        return carry

    def second(f, carry):
        @pl.when(f < ahead)
        def _():
            middle(f + chunks - ahead, 0)

        return backward(f, carry)

    lax.fori_loop(0, chunks, first, 0)
    lax.fori_loop(0, chunks, second, 0)
    lax.fori_loop(0, chunks, event_grads, 0)
    lax.fori_loop(0, chunks, finish, 0)
    with jax.named_scope("drain"):
        for ph in range(4):
            sent(ph)


def lay_out(small_in, dkeys, dvalues, layer_out, grad_queries, grad_gate, out_keys, out_values,
            joined, sem):
    chunks, users, events = dkeys.shape[:3]
    depth = joined.shape[0]
    blocks = [(i, j) for j in range(0, events, MERGE) for i in range(2)]

    def store(at):
        i, j = blocks[at]
        return pltpu.make_async_copy(
            joined.at[at % depth], (out_keys, out_values)[i].at[pl.ds(j, MERGE)], sem.at[at % depth])

    for at, (i, j) in enumerate(blocks):
        if at >= depth:
            store(at - depth).wait()
        for f in range(chunks):
            parts = [(dkeys, dvalues)[i][f, u, j:j + MERGE] for u in range(users)]
            joined[at % depth, :, :, lanes(f)] = jnp.concatenate(parts, axis=1).reshape(
                MERGE, users, PAIR)
        store(at).start()
    for i, out in enumerate((layer_out, grad_queries, grad_gate)):
        for f in range(chunks):
            out[:, :, lanes(f)] = jnp.swapaxes(small_in[i, f], 0, 1)
    for at in range(max(0, len(blocks) - depth), len(blocks)):
        store(at).wait()


def body(n, queries, gate_pre, event_keys, event_values, block_lists, history_len, out_grad):
    rows, users, width = queries.shape
    events = event_keys.shape[0]
    chunks = width // PAIR
    latents = n * rows
    vmem = pl.BlockSpec(memory_space=pltpu.VMEM)
    smem = pl.BlockSpec(memory_space=pltpu.SMEM)
    hbm = pl.BlockSpec(memory_space=pl.ANY)
    table = [pltpu.SMEM((n, SLOTS), jnp.int32), pltpu.SMEM((n, users), jnp.int32)]
    flops = 6 * 2 * users * width * latents * events
    packed = (chunks, users, events, PAIR)
    small_out, dkeys, dvalues = pl.pallas_call(
        functools.partial(kernel, n, chunks),
        out_shape=(
            pltpu.VMEM((3, chunks, users, rows, PAIR), BF16),
            pltpu.VMEM(packed, BF16),
            pltpu.VMEM(packed, BF16),
        ),
        in_specs=[smem, smem, vmem, vmem, vmem, hbm, hbm],
        out_specs=(vmem, vmem, vmem),
        scratch_shapes=[
            pltpu.VMEM((2, 2, events, users, PAIR), BF16),
            pltpu.VMEM((SPLIT * users, PAIR), F32),
            pltpu.VMEM((3, chunks, users, rows, PAIR), BF16),
            pltpu.VMEM(packed, BF16),
            pltpu.VMEM(packed, BF16),
            pltpu.VMEM((chunks, users, 2 * latents // PAIR, events, PAIR), BF16),
            pltpu.VMEM((chunks, users, 2 * latents // PAIR, events, PAIR), BF16),
            pltpu.VMEM((chunks, users, latents, PAIR), BF16),
            pltpu.VMEM((chunks, users, latents, PAIR), BF16),
            pltpu.VMEM((chunks, users, n, rows, PAIR), BF16),
            pltpu.VMEM((chunks, users, rows, PAIR), BF16),
            pltpu.VMEM((n, SLOTS + 1, rows, PAIR), BF16),
            pltpu.VMEM((4, chunks, n, SLOTS, rows, PAIR), BF16),
            pltpu.VMEM((4, chunks, n, SLOTS, rows, PAIR), BF16),
            *table,
            *table,
            pltpu.SemaphoreType.DMA((4,)),
            pltpu.SemaphoreType.DMA((4, chunks)),
            pltpu.SemaphoreType.DMA((2, chunks)),
        ],
        compiler_params=pltpu.CompilerParams(
            collective_id=0, has_side_effects=True, vmem_limit_bytes=54 * 1024 * 1024
        ),
        cost_estimate=pl.CostEstimate(
            flops=flops, bytes_accessed=8 * users * events * width, transcendentals=0),
        name="sparse_attention",
    )(block_lists.transpose(1, 2, 0), history_len, queries, gate_pre, out_grad,
      event_keys, event_values)

    tiny = jax.ShapeDtypeStruct((rows, users, width), BF16)
    large = jax.ShapeDtypeStruct((events, users, width), BF16)
    return pl.pallas_call(
        lay_out,
        out_shape=(tiny, tiny, tiny, large, large),
        in_specs=[vmem, vmem, vmem],
        out_specs=(vmem, vmem, vmem, hbm, hbm),
        scratch_shapes=[
            pltpu.VMEM((4, MERGE, users, width), BF16),
            pltpu.SemaphoreType.DMA((4,)),
        ],
        compiler_params=pltpu.CompilerParams(vmem_limit_bytes=16 * 1024 * 1024),
        cost_estimate=pl.CostEstimate(
            flops=0, bytes_accessed=8 * users * events * width, transcendentals=0),
        name="lay_out",
    )(*(pltpu.with_memory_space_constraint(x, pltpu.VMEM) for x in (small_out, dkeys, dvalues)))


def solution(mesh):
    shard = P("seq", "dp", "head")
    return jax.shard_map(
        functools.partial(body, mesh.shape["seq"]),
        mesh=mesh,
        in_specs=(shard, shard, shard, shard, P(None, "dp", None), P("dp"), shard),
        out_specs=(shard,) * 5,
        check_vma=False,
    )
```

```python
import functools

import jax
import jax.numpy as jnp
from jax import lax
from jax.experimental import pallas as pl
from jax.experimental.pallas import tpu as pltpu
from jax.sharding import PartitionSpec as P

HEAD_DIM = 64
EPS = 1e-06
SLOTS = 2
PAIR = 2 * HEAD_DIM
TILE = 256
SPLIT = 256
MERGE = 128
F32 = jnp.float32
BF16 = jnp.bfloat16
NT = (((1,), (1,)), ((), ()))
NN = (((1,), (0,)), ((), ()))
MESH = pl.DeviceIdType.MESH


def dot(a, b, dims):
    return lax.dot_general(a, b, dims, preferred_element_type=F32)


def split_heads(rows):
    lane = lax.broadcasted_iota(jnp.int32, rows.shape, 1)
    zero = jnp.zeros_like(rows)
    return jnp.concatenate(
        [jnp.where(lane < HEAD_DIM, rows, zero), jnp.where(lane < HEAD_DIM, zero, rows)], axis=0
    )


def join_heads(flipped):
    half = flipped.shape[1] // 2
    return jnp.concatenate([flipped[:HEAD_DIM, :half], flipped[HEAD_DIM:, half:]], axis=0).T


def lanes(f):
    return slice(f * PAIR, (f + 1) * PAIR)


def kernel(n, chunks, all_lists, all_lens, queries, gates, grads, keys, values,
           small_out, k_buf, v_buf,
           lists, lens, given, raw, mixed, small, w_buf, s_buf,
           q_dense, d_dense, a_dense, d_own, stage,
           sends, recvs,
           user_hold, slot_hold, user_own, slot_own,
           send_sem, recv_sem, load_sem, given_sem):
    users, events = k_buf.shape[1:3]
    rows = queries.shape[0]
    latents = n * rows
    pieces = 2 * latents // PAIR
    me = lax.axis_index("seq")

    barrier = pltpu.get_barrier_semaphore()
    for d in range(1, n):
        pl.semaphore_signal(barrier, inc=1, device_id={"seq": lax.rem(me + d, n)},
                            device_id_type=MESH)

    def given_copy(i):
        source = (all_lists, all_lens, queries, gates, grads)[i]
        target = (lists, lens, given.at[0], given.at[1], given.at[2])[i]
        return pltpu.make_async_copy(source, target, given_sem.at[i])

    for i in range(5):
        given_copy(i).start()

    def load_copy(i, f):
        at = pl.ds(pl.multiple_of(f * PAIR, PAIR), PAIR)
        return pltpu.make_async_copy(
            (keys, values)[i].at[:, :, at], raw.at[i, lax.rem(f, 2)], load_sem.at[i, f])

    for f in range(min(2, chunks)):
        load_copy(0, f).start()
        load_copy(1, f).start()

    def tables(own, p, carry):
        for user_of, slot_of, span, block in (
            ((user_own, slot_own, me, p),) if own else ((user_hold, slot_hold, p, me),)
        ):
            offset = lax.rem(span - block + n, n)
            count = jnp.int32(0)
            named = [jnp.int32(0)] * SLOTS
            for u in range(users):
                hit = lists[u, 0, span] == offset
                for i in range(1, lists.shape[1]):
                    hit = hit | (lists[u, i, span] == offset)
                hit = hit & (block < lens[u])
                slot_of[p, u] = jnp.where(hit, count, SLOTS)
                for s in range(SLOTS):
                    named[s] = jnp.where(hit & (count == s), u, named[s])
                count = count + jnp.where(hit, 1, 0)
            for s in range(SLOTS):
                user_of[p, s] = named[s]
        return carry

    given_copy(0).wait()
    given_copy(1).wait()
    lax.fori_loop(0, n, functools.partial(tables, True), 0)

    def sort_users(i, scale=None):
        given_copy(i + 2).wait()
        whole = given[i] if scale is None else (given[i] * scale).astype(BF16)
        for f in range(chunks):
            small[i, f] = jnp.swapaxes(whole[:, :, lanes(f)], 0, 1)

    sort_users(0, 0.0625)

    def copy(ph, f, to, slot):
        return pltpu.make_async_remote_copy(
            src_ref=sends.at[ph, f, to], dst_ref=recvs.at[ph, f, slot],
            send_sem=send_sem.at[ph], recv_sem=recv_sem.at[ph, f],
            device_id={"seq": to}, device_id_type=MESH)

    def exchange(ph, f, read, user_of):
        for s in range(SLOTS):
            recvs[ph, f, me, s] = read(user_of[me, s], me)

        for d in range(1, n):
            to = lax.rem(me + d, n)
            for s in range(SLOTS):
                sends[ph, f, to, s] = read(user_of[to, s], to)
            copy(ph, f, to, me).start()

    def arrive(ph, f):
        every = pl.ds(0, n - 1)
        pltpu.make_async_remote_copy(
            src_ref=sends.at[ph, f, every], dst_ref=recvs.at[ph, f, every],
            send_sem=send_sem.at[ph], recv_sem=recv_sem.at[ph, f],
            device_id={"seq": lax.rem(me + 1, n)}, device_id_type=MESH).wait_recv()

    def sent(ph):
        ref = sends.at[ph, :, pl.ds(0, n - 1)]
        pltpu.make_async_remote_copy(
            src_ref=ref, dst_ref=ref, send_sem=send_sem.at[ph], recv_sem=recv_sem.at[ph, 0],
            device_id={"seq": lax.rem(me + 1, n)}, device_id_type=MESH).wait_send()

    def spread(read, slot_of, dense):
        for p in range(n):
            for s in range(SLOTS):
                stage[p, s] = read(p, s)
        for u in range(users):
            for p in range(n):
                dense[u, p * rows:(p + 1) * rows] = stage[p, slot_of[p, u]]

    def gathered(ph, f, slot_of):
        for p in range(n):
            for s in range(SLOTS):
                stage[p, s] = recvs[ph, f, p, s]
        out = []
        for u in range(users):
            total = stage[0, slot_of[0, u]].astype(F32)
            for p in range(1, n):
                total = total + stage[p, slot_of[p, u]].astype(F32)
            out.append(total)
        return jnp.concatenate(out, axis=0)

    def flipped(buf, f, u):
        return jnp.concatenate(
            [buf[f, u, j:j + PAIR].T for j in range(0, events, PAIR)], axis=1)

    def wide(buf, f, u, tile):
        return jnp.concatenate([buf[f, u, h, tile] for h in range(pieces)], axis=1)

    def prepare(f):
        for i, buf in enumerate((k_buf, v_buf)):
            load_copy(i, f).wait()

            def split(g, carry):
                at = pl.ds(pl.multiple_of(g * SPLIT, SPLIT), SPLIT)
                mixed[...] = raw[i, lax.rem(f, 2), at].astype(F32).reshape(SPLIT * users, PAIR)
                for u in range(users):
                    buf[f, u, at] = mixed[pl.ds(u, SPLIT, users), :].astype(BF16)
                return carry

            with jax.named_scope("split"):
                lax.fori_loop(0, events // SPLIT, split, 0)

            @pl.when(f + 2 < chunks)
            def _():
                load_copy(i, f + 2).start()

    def forward(f, carry):
        with jax.named_scope("wait_queries"):
            arrive(0, f)
        with jax.named_scope("spread_queries"):
            spread(lambda p, s: recvs[0, f, p, s], slot_hold, q_dense.at[f])
        with jax.named_scope("attend"):
            for u in range(users):
                query = split_heads(q_dense[f, u])
                for j in range(0, events, TILE):
                    score = dot(k_buf[f, u, j:j + TILE], query, NT)
                    half = score.astype(BF16)
                    bent = jnp.tanh(score).astype(BF16)
                    weight = half * (1.0 + bent)
                    for h in range(pieces):
                        w_buf[f, u, h, j:j + TILE] = weight[:, lanes(h)]
                        s_buf[f, u, h, j:j + TILE] = bent[:, lanes(h)]
            for u in range(users):
                a_dense[f, u] = join_heads(
                    dot(flipped(v_buf, f, u), wide(w_buf, f, u, slice(None)), NN).astype(BF16)
                ).reshape(n, rows, PAIR)
        with jax.named_scope("send_attended"):
            exchange(1, f, lambda u, c: a_dense[f, u, c], user_hold)
        return carry

    def slopes(f):
        with jax.named_scope("slopes"):
            for u in range(users):
                for h in range(pieces):
                    bent, weight = s_buf[f, u, h], w_buf[f, u, h]
                    s_buf[f, u, h] = (1.0 + bent) + weight * (1.0 - bent)

    lane_a = lax.broadcasted_iota(jnp.int32, (PAIR, PAIR), 0) // HEAD_DIM
    lane_b = lax.broadcasted_iota(jnp.int32, (PAIR, PAIR), 1) // HEAD_DIM

    def middle(f, carry):
        averager = jnp.where(lane_a == lane_b, 1.0 / HEAD_DIM, 0.0).astype(F32)

        def head_mean(x):
            return lax.dot_general(x, averager, NN, preferred_element_type=F32,
                                   precision=lax.Precision.HIGHEST)

        with jax.named_scope("wait_attended"):
            arrive(1, f)
        with jax.named_scope("middle"):
            attended = gathered(1, f, slot_own)
            gate = small[1, f].reshape(users * rows, PAIR).astype(F32)
            grad = small[2, f].reshape(users * rows, PAIR).astype(F32)
            root = lax.rsqrt(head_mean(attended * attended) + EPS)
            normed = attended * root
            logistic = jax.nn.sigmoid(gate)
            gate_silu = gate * logistic
            slope = logistic * (1.0 + gate * (1.0 - logistic))
            shape = (users, rows, PAIR)
            small_out[0, f] = (normed * gate_silu).astype(BF16).reshape(shape)
            small_out[2, f] = (grad * normed * slope).astype(BF16).reshape(shape)
            grad_normed = grad * gate_silu
            back = root * (grad_normed - normed * head_mean(grad_normed * normed))
            d_own[f] = back.astype(BF16).reshape(shape)
            exchange(2, f, lambda u, c: d_own[f, u], user_own)
        return carry

    def backward(f, carry):
        with jax.named_scope("wait_grads"):
            arrive(2, f)
        with jax.named_scope("spread_grads"):
            spread(lambda p, s: recvs[2, f, p, s], slot_hold, d_dense.at[f])
        with jax.named_scope("query_grads"):
            grads_of = [split_heads(d_dense[f, u]) for u in range(users)]
            grad_scores = [[] for _ in range(users)]
            for j in range(0, events, TILE):
                for u in range(users):
                    grad_weight = dot(v_buf[f, u, j:j + TILE], grads_of[u], NT).astype(BF16)
                    grad_score = grad_weight * wide(s_buf, f, u, slice(j, j + TILE))
                    grad_scores[u].append(grad_score)
                    for h in range(pieces):
                        s_buf[f, u, h, j:j + TILE] = grad_score[:, lanes(h)]
            for u in range(users):
                a_dense[f, u] = join_heads(
                    (dot(flipped(k_buf, f, u), jnp.concatenate(grad_scores[u], axis=0), NN)
                     * 0.0625).astype(BF16)
                ).reshape(n, rows, PAIR)
        with jax.named_scope("send_query_grads"):
            exchange(3, f, lambda u, c: a_dense[f, u, c], user_hold)
        return carry

    def event_grads(f, carry):
        with jax.named_scope("event_grads"):
            for u in range(users):
                query = split_heads(q_dense[f, u])
                grad = split_heads(d_dense[f, u])
                for j in range(0, events, TILE):
                    tile = slice(j, j + TILE)
                    v_buf[f, u, tile] = dot(wide(w_buf, f, u, tile), grad, NN).astype(BF16)
                    k_buf[f, u, tile] = dot(wide(s_buf, f, u, tile), query, NN).astype(BF16)
        return carry

    def finish(f, carry):
        with jax.named_scope("wait_query_grads"):
            arrive(3, f)
        with jax.named_scope("finish"):
            small_out[1, f] = gathered(3, f, slot_own).astype(BF16).reshape(users, rows, PAIR)
        return carry

    prepare(0)
    with jax.named_scope("barrier"):
        pl.semaphore_wait(barrier, n - 1)
    for p in range(n):
        stage[p, SLOTS] = jnp.zeros((rows, PAIR), BF16)

    def opening(f, carry):
        with jax.named_scope("send_queries"):
            exchange(0, f, lambda u, c: small[0, f, u], user_own)

        @pl.when(f == 0)
        def _():
            lax.fori_loop(0, n, functools.partial(tables, False), 0)
            sort_users(1)
            sort_users(2)

        @pl.when(f + 1 < chunks)
        def _():
            prepare(f + 1)

        return carry

    def between(f, carry):
        @pl.when(f + 1 < chunks)
        def _():
            slopes(f + 1)

        return middle(f, carry)

    lax.fori_loop(0, chunks, opening, 0)
    lax.fori_loop(0, chunks, forward, 0)
    slopes(0)
    lax.fori_loop(0, chunks, between, 0)
    lax.fori_loop(0, chunks, backward, 0)
    lax.fori_loop(0, chunks, event_grads, 0)
    lax.fori_loop(0, chunks, finish, 0)
    with jax.named_scope("drain"):
        for ph in range(4):
            sent(ph)


def lay_out(small_in, dkeys, dvalues, layer_out, grad_queries, grad_gate, out_keys, out_values,
            joined, tiny, sem, tiny_sem):
    chunks, users, events = dkeys.shape[:3]
    depth = joined.shape[0]
    blocks = [(i, j) for j in range(0, events, MERGE) for i in range(2)]

    def store(at):
        i, j = blocks[at]
        return pltpu.make_async_copy(
            joined.at[at % depth], (out_keys, out_values)[i].at[pl.ds(j, MERGE)], sem.at[at % depth])

    def store_tiny(i):
        return pltpu.make_async_copy(
            tiny.at[i], (layer_out, grad_queries, grad_gate)[i], tiny_sem.at[i])

    for at, (i, j) in enumerate(blocks):
        if at >= depth:
            store(at - depth).wait()
        for f in range(chunks):
            parts = [(dkeys, dvalues)[i][f, u, j:j + MERGE] for u in range(users)]
            joined[at % depth, :, :, lanes(f)] = jnp.concatenate(parts, axis=1).reshape(
                MERGE, users, PAIR)
        store(at).start()
        if at == 2:
            for k in range(3):
                for f in range(chunks):
                    tiny[k, :, :, lanes(f)] = jnp.swapaxes(small_in[k, f], 0, 1)
                store_tiny(k).start()
    for k in range(3):
        store_tiny(k).wait()
    for at in range(max(0, len(blocks) - depth), len(blocks)):
        store(at).wait()


def body(n, queries, gate_pre, event_keys, event_values, block_lists, history_len, out_grad):
    rows, users, width = queries.shape
    events = event_keys.shape[0]
    chunks = width // PAIR
    latents = n * rows
    vmem = pl.BlockSpec(memory_space=pltpu.VMEM)
    hbm = pl.BlockSpec(memory_space=pl.ANY)
    table = [pltpu.SMEM((n, SLOTS), jnp.int32), pltpu.SMEM((n, users), jnp.int32)]
    flops = 6 * 2 * users * width * latents * events
    lists = block_lists.transpose(1, 2, 0)
    packed = (chunks, users, events, PAIR)
    dense = (chunks, users, latents, PAIR)
    square = (chunks, users, 2 * latents // PAIR, events, PAIR)
    outs = (pltpu.VMEM((3, chunks, users, rows, PAIR), BF16), pltpu.VMEM(packed, BF16),
            pltpu.VMEM(packed, BF16))
    kept = pl.pallas_call(
        functools.partial(kernel, n, chunks),
        out_shape=outs,
        in_specs=[hbm] * 7,
        out_specs=(vmem,) * len(outs),
        scratch_shapes=[
            pltpu.SMEM(lists.shape, jnp.int32),
            pltpu.SMEM(history_len.shape, jnp.int32),
            pltpu.VMEM((3, rows, users, width), BF16),
            pltpu.VMEM((2, 2, events, users, PAIR), BF16),
            pltpu.VMEM((SPLIT * users, PAIR), F32),
            pltpu.VMEM((3, chunks, users, rows, PAIR), BF16),
            pltpu.VMEM(square, BF16),
            pltpu.VMEM(square, BF16),
            pltpu.VMEM(dense, BF16),
            pltpu.VMEM(dense, BF16),
            pltpu.VMEM((chunks, users, n, rows, PAIR), BF16),
            pltpu.VMEM((chunks, users, rows, PAIR), BF16),
            pltpu.VMEM((n, SLOTS + 1, rows, PAIR), BF16),
            pltpu.VMEM((4, chunks, n, SLOTS, rows, PAIR), BF16),
            pltpu.VMEM((4, chunks, n, SLOTS, rows, PAIR), BF16),
            *table,
            *table,
            pltpu.SemaphoreType.DMA((4,)),
            pltpu.SemaphoreType.DMA((4, chunks)),
            pltpu.SemaphoreType.DMA((2, chunks)),
            pltpu.SemaphoreType.DMA((5,)),
        ],
        compiler_params=pltpu.CompilerParams(
            collective_id=0, has_side_effects=True, vmem_limit_bytes=54 * 1024 * 1024
        ),
        cost_estimate=pl.CostEstimate(
            flops=flops, bytes_accessed=8 * users * events * width, transcendentals=0),
        name="sparse_attention",
    )(*(pltpu.with_memory_space_constraint(x, pltpu.HBM) for x in (
        lists, history_len, queries, gate_pre, out_grad, event_keys, event_values)))

    tiny = jax.ShapeDtypeStruct((rows, users, width), BF16)
    large = jax.ShapeDtypeStruct((events, users, width), BF16)
    return pl.pallas_call(
        lay_out,
        out_shape=(tiny, tiny, tiny, large, large),
        in_specs=[vmem] * len(outs),
        out_specs=(hbm,) * 5,
        scratch_shapes=[
            pltpu.VMEM((4, MERGE, users, width), BF16),
            pltpu.VMEM((3, rows, users, width), BF16),
            pltpu.SemaphoreType.DMA((4,)),
            pltpu.SemaphoreType.DMA((3,)),
        ],
        compiler_params=pltpu.CompilerParams(vmem_limit_bytes=16 * 1024 * 1024),
        cost_estimate=pl.CostEstimate(
            flops=0, bytes_accessed=8 * users * events * width, transcendentals=0),
        name="lay_out",
    )(*(pltpu.with_memory_space_constraint(x, pltpu.VMEM) for x in kept))


def solution(mesh):
    shard = P("seq", "dp", "head")
    return jax.shard_map(
        functools.partial(body, mesh.shape["seq"]),
        mesh=mesh,
        in_specs=(shard, shard, shard, shard, P(None, "dp", None), P("dp"), shard),
        out_specs=(shard,) * 5,
        check_vma=False,
    )
```

```python
import functools

import jax
import jax.numpy as jnp
from jax import lax
from jax.experimental import pallas as pl
from jax.experimental.pallas import tpu as pltpu
from jax.sharding import PartitionSpec as P

HEAD_DIM = 64
EPS = 1e-06
SLOTS = 2
PAIR = 2 * HEAD_DIM
TILE = 256
SPLIT = 256
MERGE = 128
F32 = jnp.float32
BF16 = jnp.bfloat16
NT = (((1,), (1,)), ((), ()))
NN = (((1,), (0,)), ((), ()))
MESH = pl.DeviceIdType.MESH


def dot(a, b, dims):
    return lax.dot_general(a, b, dims, preferred_element_type=F32)


def split_heads(rows):
    lane = lax.broadcasted_iota(jnp.int32, rows.shape, 1)
    zero = jnp.zeros_like(rows)
    return jnp.concatenate(
        [jnp.where(lane < HEAD_DIM, rows, zero), jnp.where(lane < HEAD_DIM, zero, rows)], axis=0
    )


def join_heads(flipped):
    half = flipped.shape[1] // 2
    return jnp.concatenate([flipped[:HEAD_DIM, :half], flipped[HEAD_DIM:, half:]], axis=0).T


def lanes(f):
    return slice(f * PAIR, (f + 1) * PAIR)


def kernel(n, chunks, all_lists, all_lens, queries, gates, grads, keys, values,
           small_out, k_buf, v_buf,
           lists, lens, given, raw, mixed, small, t_buf, w_buf, s_buf,
           q_dense, d_dense, a_dense, d_own, stage,
           sends, recvs,
           user_hold, slot_hold, user_own, slot_own,
           send_sem, recv_sem, load_sem, given_sem):
    users, events = k_buf.shape[1:3]
    rows = queries.shape[0]
    latents = n * rows
    pieces = 2 * latents // PAIR
    me = lax.axis_index("seq")

    barrier = pltpu.get_barrier_semaphore()
    for d in range(1, n):
        pl.semaphore_signal(barrier, inc=1, device_id={"seq": lax.rem(me + d, n)},
                            device_id_type=MESH)

    def given_copy(i):
        source = (all_lists, all_lens, queries, gates, grads)[i]
        target = (lists, lens, given.at[0], given.at[1], given.at[2])[i]
        return pltpu.make_async_copy(source, target, given_sem.at[i])

    for i in range(5):
        given_copy(i).start()

    def load_copy(i, f):
        at = pl.ds(pl.multiple_of(f * PAIR, PAIR), PAIR)
        return pltpu.make_async_copy(
            (keys, values)[i].at[:, :, at], raw.at[i, lax.rem(f, 2)], load_sem.at[i, f])

    for f in range(min(2, chunks)):
        load_copy(0, f).start()
        load_copy(1, f).start()

    def tables(own, p, carry):
        for user_of, slot_of, span, block in (
            ((user_own, slot_own, me, p),) if own else ((user_hold, slot_hold, p, me),)
        ):
            offset = lax.rem(span - block + n, n)
            count = jnp.int32(0)
            named = [jnp.int32(0)] * SLOTS
            for u in range(users):
                hit = lists[u, 0, span] == offset
                for i in range(1, lists.shape[1]):
                    hit = hit | (lists[u, i, span] == offset)
                hit = hit & (block < lens[u])
                slot_of[p, u] = jnp.where(hit, count, SLOTS)
                for s in range(SLOTS):
                    named[s] = jnp.where(hit & (count == s), u, named[s])
                count = count + jnp.where(hit, 1, 0)
            for s in range(SLOTS):
                user_of[p, s] = named[s]
        return carry

    given_copy(0).wait()
    given_copy(1).wait()
    lax.fori_loop(0, n, functools.partial(tables, True), 0)

    def sort_users(i, scale=None):
        given_copy(i + 2).wait()
        whole = given[i] if scale is None else (given[i] * scale).astype(BF16)
        for f in range(chunks):
            small[i, f] = jnp.swapaxes(whole[:, :, lanes(f)], 0, 1)

    sort_users(0, 0.0625)

    def copy(ph, f, to, slot):
        return pltpu.make_async_remote_copy(
            src_ref=sends.at[ph, f, to], dst_ref=recvs.at[ph, f, slot],
            send_sem=send_sem.at[ph], recv_sem=recv_sem.at[ph, f],
            device_id={"seq": to}, device_id_type=MESH)

    def exchange(ph, f, read, user_of):
        for s in range(SLOTS):
            recvs[ph, f, me, s] = read(user_of[me, s], me)

        for d in range(1, n):
            to = lax.rem(me + d, n)
            for s in range(SLOTS):
                sends[ph, f, to, s] = read(user_of[to, s], to)
            copy(ph, f, to, me).start()

    def arrive(ph, f):
        every = pl.ds(0, n - 1)
        pltpu.make_async_remote_copy(
            src_ref=sends.at[ph, f, every], dst_ref=recvs.at[ph, f, every],
            send_sem=send_sem.at[ph], recv_sem=recv_sem.at[ph, f],
            device_id={"seq": lax.rem(me + 1, n)}, device_id_type=MESH).wait_recv()

    def sent(ph):
        ref = sends.at[ph, :, pl.ds(0, n - 1)]
        pltpu.make_async_remote_copy(
            src_ref=ref, dst_ref=ref, send_sem=send_sem.at[ph], recv_sem=recv_sem.at[ph, 0],
            device_id={"seq": lax.rem(me + 1, n)}, device_id_type=MESH).wait_send()

    def spread(read, slot_of, dense):
        for p in range(n):
            for s in range(SLOTS):
                stage[p, s] = read(p, s)
        for u in range(users):
            for p in range(n):
                dense[u, p * rows:(p + 1) * rows] = stage[p, slot_of[p, u]]

    def gathered(ph, f, slot_of):
        for p in range(n):
            for s in range(SLOTS):
                stage[p, s] = recvs[ph, f, p, s]
        out = []
        for u in range(users):
            total = stage[0, slot_of[0, u]].astype(F32)
            for p in range(1, n):
                total = total + stage[p, slot_of[p, u]].astype(F32)
            out.append(total)
        return jnp.concatenate(out, axis=0)

    def flip(buf, f):
        with jax.named_scope("flip"):
            for u in range(users):
                for j in range(events // PAIR):
                    t_buf[f, u, j] = buf[f, u, j * PAIR:(j + 1) * PAIR].T

    def flipped(f, u):
        return jnp.concatenate([t_buf[f, u, j] for j in range(events // PAIR)], axis=1)

    def wide(buf, f, u, tile):
        return jnp.concatenate([buf[f, u, h, tile] for h in range(pieces)], axis=1)

    def prepare(f):
        for i, buf in enumerate((k_buf, v_buf)):
            load_copy(i, f).wait()

            def split(g, carry):
                at = pl.ds(pl.multiple_of(g * SPLIT, SPLIT), SPLIT)
                mixed[...] = raw[i, lax.rem(f, 2), at].astype(F32).reshape(SPLIT * users, PAIR)
                for u in range(users):
                    buf[f, u, at] = mixed[pl.ds(u, SPLIT, users), :].astype(BF16)
                return carry

            with jax.named_scope("split"):
                lax.fori_loop(0, events // SPLIT, split, 0)

            @pl.when(f + 2 < chunks)
            def _():
                load_copy(i, f + 2).start()

        flip(v_buf, f)

    def forward(f, carry):
        with jax.named_scope("wait_queries"):
            arrive(0, f)
        with jax.named_scope("spread_queries"):
            spread(lambda p, s: recvs[0, f, p, s], slot_hold, q_dense.at[f])
        with jax.named_scope("attend"):
            for u in range(users):
                query = split_heads(q_dense[f, u])
                for j in range(0, events, TILE):
                    score = dot(k_buf[f, u, j:j + TILE], query, NT)
                    half = score.astype(BF16)
                    bent = jnp.tanh(score).astype(BF16)
                    weight = half * (1.0 + bent)
                    for h in range(pieces):
                        w_buf[f, u, h, j:j + TILE] = weight[:, lanes(h)]
                        s_buf[f, u, h, j:j + TILE] = bent[:, lanes(h)]
            for u in range(users):
                a_dense[f, u] = join_heads(
                    dot(flipped(f, u), wide(w_buf, f, u, slice(None)), NN).astype(BF16)
                ).reshape(n, rows, PAIR)
        with jax.named_scope("send_attended"):
            exchange(1, f, lambda u, c: a_dense[f, u, c], user_hold)
        return carry

    def slopes(f):
        with jax.named_scope("slopes"):
            for u in range(users):
                for h in range(pieces):
                    for j in range(0, events, PAIR):
                        tile = slice(j, j + PAIR)
                        bent, weight = s_buf[f, u, h, tile], w_buf[f, u, h, tile]
                        s_buf[f, u, h, tile] = (1.0 + bent) + weight * (1.0 - bent)

    lane_a = lax.broadcasted_iota(jnp.int32, (PAIR, PAIR), 0) // HEAD_DIM
    lane_b = lax.broadcasted_iota(jnp.int32, (PAIR, PAIR), 1) // HEAD_DIM

    def middle(f, carry):
        averager = jnp.where(lane_a == lane_b, 1.0 / HEAD_DIM, 0.0).astype(BF16)

        def head_mean(x):
            high = x.astype(BF16)
            low = (x - high.astype(F32)).astype(BF16)
            return dot(high, averager, NN) + dot(low, averager, NN)

        with jax.named_scope("wait_attended"):
            arrive(1, f)
        with jax.named_scope("middle"):
            attended = gathered(1, f, slot_own)
            gate = small[1, f].reshape(users * rows, PAIR).astype(F32)
            grad = small[2, f].reshape(users * rows, PAIR).astype(F32)
            root = lax.rsqrt(head_mean(attended * attended) + EPS)
            normed = attended * root
            logistic = jax.nn.sigmoid(gate)
            gate_silu = gate * logistic
            slope = logistic * (1.0 + gate * (1.0 - logistic))
            shape = (users, rows, PAIR)
            small_out[0, f] = (normed * gate_silu).astype(BF16).reshape(shape)
            small_out[2, f] = (grad * normed * slope).astype(BF16).reshape(shape)
            grad_normed = grad * gate_silu
            back = root * (grad_normed - normed * head_mean(grad_normed * normed))
            d_own[f] = back.astype(BF16).reshape(shape)
            exchange(2, f, lambda u, c: d_own[f, u], user_own)
        return carry

    def backward(f, carry):
        with jax.named_scope("wait_grads"):
            arrive(2, f)
        with jax.named_scope("spread_grads"):
            spread(lambda p, s: recvs[2, f, p, s], slot_hold, d_dense.at[f])
        with jax.named_scope("query_grads"):
            grads_of = [split_heads(d_dense[f, u]) for u in range(users)]
            grad_scores = [[] for _ in range(users)]
            for j in range(0, events, TILE):
                for u in range(users):
                    grad_weight = dot(v_buf[f, u, j:j + TILE], grads_of[u], NT).astype(BF16)
                    grad_score = grad_weight * wide(s_buf, f, u, slice(j, j + TILE))
                    grad_scores[u].append(grad_score)
                    for h in range(pieces):
                        s_buf[f, u, h, j:j + TILE] = grad_score[:, lanes(h)]
            for u in range(users):
                a_dense[f, u] = join_heads(
                    (dot(flipped(f, u), jnp.concatenate(grad_scores[u], axis=0), NN)
                     * 0.0625).astype(BF16)
                ).reshape(n, rows, PAIR)
        with jax.named_scope("send_query_grads"):
            exchange(3, f, lambda u, c: a_dense[f, u, c], user_hold)
        return carry

    def event_grads(f, carry):
        with jax.named_scope("event_grads"):
            for u in range(users):
                query = split_heads(q_dense[f, u])
                grad = split_heads(d_dense[f, u])
                for j in range(0, events, TILE):
                    tile = slice(j, j + TILE)
                    v_buf[f, u, tile] = dot(wide(w_buf, f, u, tile), grad, NN).astype(BF16)
                    k_buf[f, u, tile] = dot(wide(s_buf, f, u, tile), query, NN).astype(BF16)
        return carry

    def finish(f, carry):
        with jax.named_scope("wait_query_grads"):
            arrive(3, f)
        with jax.named_scope("finish"):
            small_out[1, f] = gathered(3, f, slot_own).astype(BF16).reshape(users, rows, PAIR)
        return carry

    prepare(0)
    with jax.named_scope("barrier"):
        pl.semaphore_wait(barrier, n - 1)
    for p in range(n):
        stage[p, SLOTS] = jnp.zeros((rows, PAIR), BF16)

    def send_queries(f, carry):
        exchange(0, f, lambda u, c: small[0, f, u], user_own)
        return carry

    def opening(f, carry):
        prepare(f)
        return carry

    def between(f, carry):
        middle(f, carry)

        @pl.when(f + early < chunks)
        def _():
            flip(k_buf, f + early)

        slopes(f)
        return carry

    early = min(2, chunks)

    def flip_early(f, carry):
        flip(k_buf, f)
        return carry

    with jax.named_scope("send_queries"):
        lax.fori_loop(0, chunks, send_queries, 0)
    lax.fori_loop(0, n, functools.partial(tables, False), 0)
    sort_users(1)
    sort_users(2)
    lax.fori_loop(1, chunks, opening, 0)
    lax.fori_loop(0, chunks, forward, 0)
    lax.fori_loop(0, early, flip_early, 0)
    lax.fori_loop(0, chunks, between, 0)
    lax.fori_loop(0, chunks, backward, 0)
    lax.fori_loop(0, chunks, event_grads, 0)
    lax.fori_loop(0, chunks, finish, 0)
    with jax.named_scope("drain"):
        for ph in range(4):
            sent(ph)


def lay_out(small_in, dkeys, dvalues, layer_out, grad_queries, grad_gate, out_keys, out_values,
            joined, tiny, sem, tiny_sem):
    chunks, users, events = dkeys.shape[:3]
    depth = joined.shape[0]
    blocks = [(i, j) for j in range(0, events, MERGE) for i in range(2)]

    def store(at):
        i, j = blocks[at]
        return pltpu.make_async_copy(
            joined.at[at % depth], (out_keys, out_values)[i].at[pl.ds(j, MERGE)], sem.at[at % depth])

    def store_tiny(i):
        return pltpu.make_async_copy(
            tiny.at[i], (layer_out, grad_queries, grad_gate)[i], tiny_sem.at[i])

    for at, (i, j) in enumerate(blocks):
        if at >= depth:
            store(at - depth).wait()
        for f in range(chunks):
            parts = [(dkeys, dvalues)[i][f, u, j:j + MERGE] for u in range(users)]
            joined[at % depth, :, :, lanes(f)] = jnp.concatenate(parts, axis=1).reshape(
                MERGE, users, PAIR)
        store(at).start()
        if at == 2:
            for k in range(3):
                for f in range(chunks):
                    tiny[k, :, :, lanes(f)] = jnp.swapaxes(small_in[k, f], 0, 1)
                store_tiny(k).start()
    for k in range(3):
        store_tiny(k).wait()
    for at in range(max(0, len(blocks) - depth), len(blocks)):
        store(at).wait()


def body(n, queries, gate_pre, event_keys, event_values, block_lists, history_len, out_grad):
    rows, users, width = queries.shape
    events = event_keys.shape[0]
    chunks = width // PAIR
    latents = n * rows
    vmem = pl.BlockSpec(memory_space=pltpu.VMEM)
    hbm = pl.BlockSpec(memory_space=pl.ANY)
    table = [pltpu.SMEM((n, SLOTS), jnp.int32), pltpu.SMEM((n, users), jnp.int32)]
    flops = 6 * 2 * users * width * latents * events
    lists = block_lists.transpose(1, 2, 0)
    packed = (chunks, users, events, PAIR)
    dense = (chunks, users, latents, PAIR)
    square = (chunks, users, 2 * latents // PAIR, events, PAIR)
    outs = (pltpu.VMEM((3, chunks, users, rows, PAIR), BF16), pltpu.VMEM(packed, BF16),
            pltpu.VMEM(packed, BF16))
    kept = pl.pallas_call(
        functools.partial(kernel, n, chunks),
        out_shape=outs,
        in_specs=[hbm] * 7,
        out_specs=(vmem,) * len(outs),
        scratch_shapes=[
            pltpu.SMEM(lists.shape, jnp.int32),
            pltpu.SMEM(history_len.shape, jnp.int32),
            pltpu.VMEM((3, rows, users, width), BF16),
            pltpu.VMEM((2, 2, events, users, PAIR), BF16),
            pltpu.VMEM((SPLIT * users, PAIR), F32),
            pltpu.VMEM((3, chunks, users, rows, PAIR), BF16),
            pltpu.VMEM((chunks, users, events // PAIR, PAIR, PAIR), BF16),
            pltpu.VMEM(square, BF16),
            pltpu.VMEM(square, BF16),
            pltpu.VMEM(dense, BF16),
            pltpu.VMEM(dense, BF16),
            pltpu.VMEM((chunks, users, n, rows, PAIR), BF16),
            pltpu.VMEM((chunks, users, rows, PAIR), BF16),
            pltpu.VMEM((n, SLOTS + 1, rows, PAIR), BF16),
            pltpu.VMEM((4, chunks, n, SLOTS, rows, PAIR), BF16),
            pltpu.VMEM((4, chunks, n, SLOTS, rows, PAIR), BF16),
            *table,
            *table,
            pltpu.SemaphoreType.DMA((4,)),
            pltpu.SemaphoreType.DMA((4, chunks)),
            pltpu.SemaphoreType.DMA((2, chunks)),
            pltpu.SemaphoreType.DMA((5,)),
        ],
        compiler_params=pltpu.CompilerParams(
            collective_id=0, has_side_effects=True, vmem_limit_bytes=54 * 1024 * 1024
        ),
        cost_estimate=pl.CostEstimate(
            flops=flops, bytes_accessed=8 * users * events * width, transcendentals=0),
        name="sparse_attention",
    )(*(pltpu.with_memory_space_constraint(x, pltpu.HBM) for x in (
        lists, history_len, queries, gate_pre, out_grad, event_keys, event_values)))

    tiny = jax.ShapeDtypeStruct((rows, users, width), BF16)
    large = jax.ShapeDtypeStruct((events, users, width), BF16)
    return pl.pallas_call(
        lay_out,
        out_shape=(tiny, tiny, tiny, large, large),
        in_specs=[vmem] * len(outs),
        out_specs=(hbm,) * 5,
        scratch_shapes=[
            pltpu.VMEM((4, MERGE, users, width), BF16),
            pltpu.VMEM((3, rows, users, width), BF16),
            pltpu.SemaphoreType.DMA((4,)),
            pltpu.SemaphoreType.DMA((3,)),
        ],
        compiler_params=pltpu.CompilerParams(vmem_limit_bytes=16 * 1024 * 1024),
        cost_estimate=pl.CostEstimate(
            flops=0, bytes_accessed=8 * users * events * width, transcendentals=0),
        name="lay_out",
    )(*(pltpu.with_memory_space_constraint(x, pltpu.VMEM) for x in kept))


def solution(mesh):
    shard = P("seq", "dp", "head")
    return jax.shard_map(
        functools.partial(body, mesh.shape["seq"]),
        mesh=mesh,
        in_specs=(shard, shard, shard, shard, P(None, "dp", None), P("dp"), shard),
        out_specs=(shard,) * 5,
        check_vma=False,
    )
```

```python
import functools

import jax
import jax.numpy as jnp
from jax import lax
from jax.experimental import pallas as pl
from jax.experimental.pallas import tpu as pltpu
from jax.sharding import PartitionSpec as P

HEAD_DIM = 64
EPS = 1e-06
SLOTS = 2
PAIR = 2 * HEAD_DIM
TILE = 256
SPLIT = 256
MERGE = 128
F32 = jnp.float32
BF16 = jnp.bfloat16
NT = (((1,), (1,)), ((), ()))
NN = (((1,), (0,)), ((), ()))
MESH = pl.DeviceIdType.MESH


def dot(a, b, dims):
    return lax.dot_general(a, b, dims, preferred_element_type=F32)


def split_heads(rows):
    lane = lax.broadcasted_iota(jnp.int32, rows.shape, 1)
    zero = jnp.zeros_like(rows)
    return jnp.concatenate(
        [jnp.where(lane < HEAD_DIM, rows, zero), jnp.where(lane < HEAD_DIM, zero, rows)], axis=0
    )


def join_heads(flipped):
    half = flipped.shape[1] // 2
    return jnp.concatenate([flipped[:HEAD_DIM, :half], flipped[HEAD_DIM:, half:]], axis=0).T


def lanes(f):
    return slice(f * PAIR, (f + 1) * PAIR)


def kernel(n, chunks, all_lists, all_lens, queries, gates, grads, keys, values,
           small_out, k_buf, v_buf,
           lists, lens, given, raw, mixed, small, t_buf, w_buf, s_buf,
           q_dense, d_dense, a_dense, d_own, stage,
           sends, recvs,
           user_hold, slot_hold, user_own, slot_own,
           send_sem, recv_sem, load_sem, given_sem):
    users, events = k_buf.shape[1:3]
    rows = queries.shape[0]
    latents = n * rows
    pieces = 2 * latents // PAIR
    me = lax.axis_index("seq")

    barrier = pltpu.get_barrier_semaphore()
    for d in range(1, n):
        pl.semaphore_signal(barrier, inc=1, device_id={"seq": lax.rem(me + d, n)},
                            device_id_type=MESH)

    def given_copy(i):
        source = (all_lists, all_lens, queries, gates, grads)[i]
        target = (lists, lens, given.at[0], given.at[1], given.at[2])[i]
        return pltpu.make_async_copy(source, target, given_sem.at[i])

    for i in range(5):
        given_copy(i).start()

    def load_copy(i, f):
        at = pl.ds(pl.multiple_of(f * PAIR, PAIR), PAIR)
        return pltpu.make_async_copy(
            (keys, values)[i].at[:, :, at], raw.at[i, lax.rem(f, 2)], load_sem.at[i, f])

    for f in range(min(2, chunks)):
        load_copy(0, f).start()
        load_copy(1, f).start()

    def tables(own, p, carry):
        for user_of, slot_of, span, block in (
            ((user_own, slot_own, me, p),) if own else ((user_hold, slot_hold, p, me),)
        ):
            offset = lax.rem(span - block + n, n)
            count = jnp.int32(0)
            named = [jnp.int32(0)] * SLOTS
            for u in range(users):
                hit = lists[u, 0, span] == offset
                for i in range(1, lists.shape[1]):
                    hit = hit | (lists[u, i, span] == offset)
                hit = hit & (block < lens[u])
                slot_of[p, u] = jnp.where(hit, count, SLOTS)
                for s in range(SLOTS):
                    named[s] = jnp.where(hit & (count == s), u, named[s])
                count = count + jnp.where(hit, 1, 0)
            for s in range(SLOTS):
                user_of[p, s] = named[s]
        return carry

    given_copy(0).wait()
    given_copy(1).wait()
    lax.fori_loop(0, n, functools.partial(tables, True), 0)

    def sort_users(i, scale=None):
        given_copy(i + 2).wait()
        whole = given[i] if scale is None else (given[i] * scale).astype(BF16)
        for f in range(chunks):
            small[i, f] = jnp.swapaxes(whole[:, :, lanes(f)], 0, 1)

    sort_users(0, 0.0625)

    def copy(ph, f, to, slot):
        return pltpu.make_async_remote_copy(
            src_ref=sends.at[ph, f, to], dst_ref=recvs.at[ph, f, slot],
            send_sem=send_sem.at[ph], recv_sem=recv_sem.at[ph, f],
            device_id={"seq": to}, device_id_type=MESH)

    def exchange(ph, f, read, user_of):
        for s in range(SLOTS):
            recvs[ph, f, me, s] = read(user_of[me, s], me)

        for d in range(1, n):
            to = lax.rem(me + d, n)
            for s in range(SLOTS):
                sends[ph, f, to, s] = read(user_of[to, s], to)
            copy(ph, f, to, me).start()

    def arrive(ph, f):
        every = pl.ds(0, n - 1)
        pltpu.make_async_remote_copy(
            src_ref=sends.at[ph, f, every], dst_ref=recvs.at[ph, f, every],
            send_sem=send_sem.at[ph], recv_sem=recv_sem.at[ph, f],
            device_id={"seq": lax.rem(me + 1, n)}, device_id_type=MESH).wait_recv()

    def sent(ph):
        ref = sends.at[ph, :, pl.ds(0, n - 1)]
        pltpu.make_async_remote_copy(
            src_ref=ref, dst_ref=ref, send_sem=send_sem.at[ph], recv_sem=recv_sem.at[ph, 0],
            device_id={"seq": lax.rem(me + 1, n)}, device_id_type=MESH).wait_send()

    def spread(read, slot_of, dense):
        for p in range(n):
            for s in range(SLOTS):
                stage[p, s] = read(p, s)
        for u in range(users):
            for p in range(n):
                dense[u, p * rows:(p + 1) * rows] = stage[p, slot_of[p, u]]

    def gathered(ph, f, slot_of):
        for p in range(n):
            for s in range(SLOTS):
                stage[p, s] = recvs[ph, f, p, s]
        out = []
        for u in range(users):
            total = stage[0, slot_of[0, u]].astype(F32)
            for p in range(1, n):
                total = total + stage[p, slot_of[p, u]].astype(F32)
            out.append(total)
        return jnp.concatenate(out, axis=0)

    def flip(buf, f):
        with jax.named_scope("flip"):
            for u in range(users):
                for j in range(events // PAIR):
                    t_buf[f, u, j] = buf[f, u, j * PAIR:(j + 1) * PAIR].T

    def flipped(f, u):
        return jnp.concatenate([t_buf[f, u, j] for j in range(events // PAIR)], axis=1)

    def wide(buf, f, u, tile):
        return jnp.concatenate([buf[f, u, h, tile] for h in range(pieces)], axis=1)

    def prepare(f):
        for i, buf in enumerate((k_buf, v_buf)):
            load_copy(i, f).wait()

            def split(g, carry):
                at = pl.ds(pl.multiple_of(g * SPLIT, SPLIT), SPLIT)
                mixed[...] = raw[i, lax.rem(f, 2), at].astype(F32).reshape(SPLIT * users, PAIR)
                for u in range(users):
                    buf[f, u, at] = mixed[pl.ds(u, SPLIT, users), :].astype(BF16)
                return carry

            with jax.named_scope("split"):
                lax.fori_loop(0, events // SPLIT, split, 0)

            @pl.when(f + 2 < chunks)
            def _():
                load_copy(i, f + 2).start()

        flip(v_buf, f)

    def forward(f, carry):
        with jax.named_scope("wait_queries"):
            arrive(0, f)
        with jax.named_scope("spread_queries"):
            spread(lambda p, s: recvs[0, f, p, s], slot_hold, q_dense.at[f])
        with jax.named_scope("attend"):
            for u in range(users):
                query = split_heads(q_dense[f, u])
                for j in range(0, events, TILE):
                    score = dot(k_buf[f, u, j:j + TILE], query, NT)
                    up = 1.0 + jnp.tanh(score).astype(BF16)
                    weight = score.astype(BF16) * up
                    for h in range(pieces):
                        w_buf[f, u, h, j:j + TILE] = weight[:, lanes(h)]
                        s_buf[f, u, h, j:j + TILE] = up[:, lanes(h)]
            for u in range(users):
                a_dense[f, u] = join_heads(
                    dot(flipped(f, u), wide(w_buf, f, u, slice(None)), NN).astype(BF16)
                ).reshape(n, rows, PAIR)
        with jax.named_scope("send_attended"):
            exchange(1, f, lambda u, c: a_dense[f, u, c], user_hold)
        return carry

    def slopes(f):
        with jax.named_scope("slopes"):
            for u in range(users):
                for h in range(pieces):
                    for j in range(0, events, PAIR):
                        tile = slice(j, j + PAIR)
                        up, weight = s_buf[f, u, h, tile], w_buf[f, u, h, tile]
                        s_buf[f, u, h, tile] = up + weight * (2.0 - up)

    lane_a = lax.broadcasted_iota(jnp.int32, (PAIR, PAIR), 0) // HEAD_DIM
    lane_b = lax.broadcasted_iota(jnp.int32, (PAIR, PAIR), 1) // HEAD_DIM

    def middle(f, carry):
        averager = jnp.where(lane_a == lane_b, 1.0 / HEAD_DIM, 0.0).astype(BF16)

        def head_mean(x):
            high = x.astype(BF16)
            low = (x - high.astype(F32)).astype(BF16)
            return dot(high, averager, NN) + dot(low, averager, NN)

        with jax.named_scope("wait_attended"):
            arrive(1, f)
        with jax.named_scope("middle"):
            attended = gathered(1, f, slot_own)
            gate = small[1, f].reshape(users * rows, PAIR).astype(F32)
            grad = small[2, f].reshape(users * rows, PAIR).astype(F32)
            root = lax.rsqrt(head_mean(attended * attended) + EPS)
            normed = attended * root
            logistic = jax.nn.sigmoid(gate)
            gate_silu = gate * logistic
            slope = logistic * (1.0 + gate * (1.0 - logistic))
            shape = (users, rows, PAIR)
            small_out[0, f] = (normed * gate_silu).astype(BF16).reshape(shape)
            small_out[2, f] = (grad * normed * slope).astype(BF16).reshape(shape)
            grad_normed = grad * gate_silu
            back = root * (grad_normed - normed * head_mean(grad_normed * normed))
            d_own[f] = back.astype(BF16).reshape(shape)
            exchange(2, f, lambda u, c: d_own[f, u], user_own)
        return carry

    def backward(f, carry):
        with jax.named_scope("wait_grads"):
            arrive(2, f)
        with jax.named_scope("spread_grads"):
            spread(lambda p, s: recvs[2, f, p, s], slot_hold, d_dense.at[f])
        with jax.named_scope("query_grads"):
            grads_of = [split_heads(d_dense[f, u]) for u in range(users)]
            grad_scores = [[] for _ in range(users)]
            for j in range(0, events, TILE):
                for u in range(users):
                    grad_weight = dot(v_buf[f, u, j:j + TILE], grads_of[u], NT).astype(BF16)
                    grad_score = grad_weight * wide(s_buf, f, u, slice(j, j + TILE))
                    grad_scores[u].append(grad_score)
                    for h in range(pieces):
                        s_buf[f, u, h, j:j + TILE] = grad_score[:, lanes(h)]
            for u in range(users):
                a_dense[f, u] = join_heads(
                    (dot(flipped(f, u), jnp.concatenate(grad_scores[u], axis=0), NN)
                     * 0.0625).astype(BF16)
                ).reshape(n, rows, PAIR)
        with jax.named_scope("send_query_grads"):
            exchange(3, f, lambda u, c: a_dense[f, u, c], user_hold)
        return carry

    def event_grads_of(f, some):
        with jax.named_scope("event_grads"):
            for u in some:
                query = split_heads(q_dense[f, u])
                grad = split_heads(d_dense[f, u])
                for j in range(0, events, TILE):
                    tile = slice(j, j + TILE)
                    v_buf[f, u, tile] = dot(wide(w_buf, f, u, tile), grad, NN).astype(BF16)
                    k_buf[f, u, tile] = dot(wide(s_buf, f, u, tile), query, NN).astype(BF16)

    def event_grads(f, carry):
        event_grads_of(f, range(users))
        return carry

    def finish(f, carry):
        with jax.named_scope("wait_query_grads"):
            arrive(3, f)
        with jax.named_scope("finish"):
            small_out[1, f] = gathered(3, f, slot_own).astype(BF16).reshape(users, rows, PAIR)
        return carry

    prepare(0)
    with jax.named_scope("barrier"):
        pl.semaphore_wait(barrier, n - 1)
    for p in range(n):
        stage[p, SLOTS] = jnp.zeros((rows, PAIR), BF16)

    def send_queries(f, carry):
        exchange(0, f, lambda u, c: small[0, f, u], user_own)
        return carry

    def opening(f, carry):
        prepare(f)
        return carry

    def between(f, carry):
        middle(f, carry)

        @pl.when(f + early < chunks)
        def _():
            flip(k_buf, f + early)

        slopes(f)
        return carry

    early = min(2, chunks)

    def flip_early(f, carry):
        flip(k_buf, f)
        return carry

    def second(f, carry):
        backward(f, carry)

        @pl.when(f == 0)
        def _():
            event_grads_of(0, range(users // 2))

        return carry

    with jax.named_scope("send_queries"):
        lax.fori_loop(0, chunks, send_queries, 0)
    lax.fori_loop(0, n, functools.partial(tables, False), 0)
    sort_users(1)
    sort_users(2)
    lax.fori_loop(1, chunks, opening, 0)
    lax.fori_loop(0, chunks, forward, 0)
    lax.fori_loop(0, early, flip_early, 0)
    lax.fori_loop(0, chunks, between, 0)
    lax.fori_loop(0, chunks, second, 0)
    event_grads_of(0, range(users // 2, users))
    lax.fori_loop(1, chunks, event_grads, 0)
    lax.fori_loop(0, chunks, finish, 0)
    with jax.named_scope("drain"):
        for ph in range(4):
            sent(ph)


def lay_out(small_in, dkeys, dvalues, layer_out, grad_queries, grad_gate, out_keys, out_values,
            joined, tiny, sem, tiny_sem):
    chunks, users, events = dkeys.shape[:3]
    depth = joined.shape[0]
    blocks = [(i, j) for j in range(0, events, MERGE) for i in range(2)]

    def store(at):
        i, j = blocks[at]
        return pltpu.make_async_copy(
            joined.at[at % depth], (out_keys, out_values)[i].at[pl.ds(j, MERGE)], sem.at[at % depth])

    def store_tiny(i):
        return pltpu.make_async_copy(
            tiny.at[i], (layer_out, grad_queries, grad_gate)[i], tiny_sem.at[i])

    for at, (i, j) in enumerate(blocks):
        if at >= depth:
            store(at - depth).wait()
        for f in range(chunks):
            parts = [(dkeys, dvalues)[i][f, u, j:j + MERGE] for u in range(users)]
            joined[at % depth, :, :, lanes(f)] = jnp.concatenate(parts, axis=1).reshape(
                MERGE, users, PAIR)
        store(at).start()
        if at == 2:
            for k in range(3):
                for f in range(chunks):
                    tiny[k, :, :, lanes(f)] = jnp.swapaxes(small_in[k, f], 0, 1)
                store_tiny(k).start()
    for k in range(3):
        store_tiny(k).wait()
    for at in range(max(0, len(blocks) - depth), len(blocks)):
        store(at).wait()


def body(n, queries, gate_pre, event_keys, event_values, block_lists, history_len, out_grad):
    rows, users, width = queries.shape
    events = event_keys.shape[0]
    chunks = width // PAIR
    latents = n * rows
    vmem = pl.BlockSpec(memory_space=pltpu.VMEM)
    hbm = pl.BlockSpec(memory_space=pl.ANY)
    table = [pltpu.SMEM((n, SLOTS), jnp.int32), pltpu.SMEM((n, users), jnp.int32)]
    flops = 6 * 2 * users * width * latents * events
    lists = block_lists.transpose(1, 2, 0)
    packed = (chunks, users, events, PAIR)
    dense = (chunks, users, latents, PAIR)
    square = (chunks, users, 2 * latents // PAIR, events, PAIR)
    outs = (pltpu.VMEM((3, chunks, users, rows, PAIR), BF16), pltpu.VMEM(packed, BF16),
            pltpu.VMEM(packed, BF16))
    kept = pl.pallas_call(
        functools.partial(kernel, n, chunks),
        out_shape=outs,
        in_specs=[hbm] * 7,
        out_specs=(vmem,) * len(outs),
        scratch_shapes=[
            pltpu.SMEM(lists.shape, jnp.int32),
            pltpu.SMEM(history_len.shape, jnp.int32),
            pltpu.VMEM((3, rows, users, width), BF16),
            pltpu.VMEM((2, 2, events, users, PAIR), BF16),
            pltpu.VMEM((SPLIT * users, PAIR), F32),
            pltpu.VMEM((3, chunks, users, rows, PAIR), BF16),
            pltpu.VMEM((chunks, users, events // PAIR, PAIR, PAIR), BF16),
            pltpu.VMEM(square, BF16),
            pltpu.VMEM(square, BF16),
            pltpu.VMEM(dense, BF16),
            pltpu.VMEM(dense, BF16),
            pltpu.VMEM((chunks, users, n, rows, PAIR), BF16),
            pltpu.VMEM((chunks, users, rows, PAIR), BF16),
            pltpu.VMEM((n, SLOTS + 1, rows, PAIR), BF16),
            pltpu.VMEM((4, chunks, n, SLOTS, rows, PAIR), BF16),
            pltpu.VMEM((4, chunks, n, SLOTS, rows, PAIR), BF16),
            *table,
            *table,
            pltpu.SemaphoreType.DMA((4,)),
            pltpu.SemaphoreType.DMA((4, chunks)),
            pltpu.SemaphoreType.DMA((2, chunks)),
            pltpu.SemaphoreType.DMA((5,)),
        ],
        compiler_params=pltpu.CompilerParams(
            collective_id=0, has_side_effects=True, vmem_limit_bytes=54 * 1024 * 1024
        ),
        cost_estimate=pl.CostEstimate(
            flops=flops, bytes_accessed=8 * users * events * width, transcendentals=0),
        name="sparse_attention",
    )(*(pltpu.with_memory_space_constraint(x, pltpu.HBM) for x in (
        lists, history_len, queries, gate_pre, out_grad, event_keys, event_values)))

    tiny = jax.ShapeDtypeStruct((rows, users, width), BF16)
    large = jax.ShapeDtypeStruct((events, users, width), BF16)
    return pl.pallas_call(
        lay_out,
        out_shape=(tiny, tiny, tiny, large, large),
        in_specs=[vmem] * len(outs),
        out_specs=(hbm,) * 5,
        scratch_shapes=[
            pltpu.VMEM((4, MERGE, users, width), BF16),
            pltpu.VMEM((3, rows, users, width), BF16),
            pltpu.SemaphoreType.DMA((4,)),
            pltpu.SemaphoreType.DMA((3,)),
        ],
        compiler_params=pltpu.CompilerParams(vmem_limit_bytes=16 * 1024 * 1024),
        cost_estimate=pl.CostEstimate(
            flops=0, bytes_accessed=8 * users * events * width, transcendentals=0),
        name="lay_out",
    )(*(pltpu.with_memory_space_constraint(x, pltpu.VMEM) for x in kept))


def solution(mesh):
    shard = P("seq", "dp", "head")
    return jax.shard_map(
        functools.partial(body, mesh.shape["seq"]),
        mesh=mesh,
        in_specs=(shard, shard, shard, shard, P(None, "dp", None), P("dp"), shard),
        out_specs=(shard,) * 5,
        check_vma=False,
    )
```

```python
import functools

import jax
import jax.numpy as jnp
from jax import lax
from jax.experimental import pallas as pl
from jax.experimental.pallas import tpu as pltpu
from jax.sharding import PartitionSpec as P

HEAD_DIM = 64
EPS = 1e-06
SLOTS = 2
PAIR = 2 * HEAD_DIM
TILE = 256
SPLIT = 256
MERGE = 128
F32 = jnp.float32
BF16 = jnp.bfloat16
NT = (((1,), (1,)), ((), ()))
NN = (((1,), (0,)), ((), ()))
MESH = pl.DeviceIdType.MESH


def dot(a, b, dims):
    return lax.dot_general(a, b, dims, preferred_element_type=F32)


def split_heads(rows):
    lane = lax.broadcasted_iota(jnp.int32, rows.shape, 1)
    zero = jnp.zeros_like(rows)
    return jnp.concatenate(
        [jnp.where(lane < HEAD_DIM, rows, zero), jnp.where(lane < HEAD_DIM, zero, rows)], axis=0
    )


def join_heads(flipped):
    half = flipped.shape[1] // 2
    return jnp.concatenate([flipped[:HEAD_DIM, :half], flipped[HEAD_DIM:, half:]], axis=0).T


def lanes(f):
    return slice(f * PAIR, (f + 1) * PAIR)


def kernel(n, chunks, all_lists, all_lens, queries, gates, grads, keys, values,
           small_out, k_buf, v_buf,
           lists, lens, given, raw, mixed, small, t_buf, w_buf, s_buf,
           q_dense, d_dense, a_dense, d_own, stage,
           sends, recvs,
           user_hold, slot_hold, user_own, slot_own,
           send_sem, recv_sem, load_sem, given_sem):
    users, events = k_buf.shape[1:3]
    rows = queries.shape[0]
    latents = n * rows
    pieces = 2 * latents // PAIR
    me = lax.axis_index("seq")

    barrier = pltpu.get_barrier_semaphore()
    for d in range(1, n):
        pl.semaphore_signal(barrier, inc=1, device_id={"seq": lax.rem(me + d, n)},
                            device_id_type=MESH)

    def given_copy(i):
        source = (all_lists, all_lens, queries, gates, grads)[i]
        target = (lists, lens, given.at[0], given.at[1], given.at[2])[i]
        return pltpu.make_async_copy(source, target, given_sem.at[i])

    for i in range(5):
        given_copy(i).start()

    def load_copy(i, f):
        at = pl.ds(pl.multiple_of(f * PAIR, PAIR), PAIR)
        return pltpu.make_async_copy(
            (keys, values)[i].at[:, :, at], raw.at[i, lax.rem(f, 2)], load_sem.at[i, f])

    for f in range(min(2, chunks)):
        load_copy(0, f).start()
        load_copy(1, f).start()

    def tables(own, p, carry):
        for user_of, slot_of, span, block in (
            ((user_own, slot_own, me, p),) if own else ((user_hold, slot_hold, p, me),)
        ):
            offset = lax.rem(span - block + n, n)
            count = jnp.int32(0)
            named = [jnp.int32(0)] * SLOTS
            for u in range(users):
                hit = lists[u, 0, span] == offset
                for i in range(1, lists.shape[1]):
                    hit = hit | (lists[u, i, span] == offset)
                hit = hit & (block < lens[u])
                slot_of[p, u] = jnp.where(hit, count, SLOTS)
                for s in range(SLOTS):
                    named[s] = jnp.where(hit & (count == s), u, named[s])
                count = count + jnp.where(hit, 1, 0)
            for s in range(SLOTS):
                user_of[p, s] = named[s]
        return carry

    given_copy(0).wait()
    given_copy(1).wait()
    lax.fori_loop(0, n, functools.partial(tables, True), 0)

    def sort_users(i, scale=None):
        given_copy(i + 2).wait()
        whole = given[i] if scale is None else (given[i] * scale).astype(BF16)
        for f in range(chunks):
            small[i, f] = jnp.swapaxes(whole[:, :, lanes(f)], 0, 1)

    sort_users(0, 0.0625)

    def copy(ph, f, to, slot):
        return pltpu.make_async_remote_copy(
            src_ref=sends.at[ph, f, to], dst_ref=recvs.at[ph, f, slot],
            send_sem=send_sem.at[ph], recv_sem=recv_sem.at[ph, f],
            device_id={"seq": to}, device_id_type=MESH)

    def exchange(ph, f, read, user_of):
        for s in range(SLOTS):
            recvs[ph, f, me, s] = read(user_of[me, s], me)

        for d in range(1, n):
            to = lax.rem(me + d, n)
            for s in range(SLOTS):
                sends[ph, f, to, s] = read(user_of[to, s], to)
            copy(ph, f, to, me).start()

    def arrive(ph, f):
        every = pl.ds(0, n - 1)
        pltpu.make_async_remote_copy(
            src_ref=sends.at[ph, f, every], dst_ref=recvs.at[ph, f, every],
            send_sem=send_sem.at[ph], recv_sem=recv_sem.at[ph, f],
            device_id={"seq": lax.rem(me + 1, n)}, device_id_type=MESH).wait_recv()

    def sent(ph):
        ref = sends.at[ph, :, pl.ds(0, n - 1)]
        pltpu.make_async_remote_copy(
            src_ref=ref, dst_ref=ref, send_sem=send_sem.at[ph], recv_sem=recv_sem.at[ph, 0],
            device_id={"seq": lax.rem(me + 1, n)}, device_id_type=MESH).wait_send()

    def spread(read, slot_of, dense):
        for p in range(n):
            for s in range(SLOTS):
                stage[p, s] = read(p, s)
        for u in range(users):
            for p in range(n):
                dense[u, p * rows:(p + 1) * rows] = stage[p, slot_of[p, u]]

    def gathered(ph, f, slot_of):
        for p in range(n):
            for s in range(SLOTS):
                stage[p, s] = recvs[ph, f, p, s]
        out = []
        for u in range(users):
            total = stage[0, slot_of[0, u]].astype(F32)
            for p in range(1, n):
                total = total + stage[p, slot_of[p, u]].astype(F32)
            out.append(total)
        return jnp.concatenate(out, axis=0)

    def flip(buf, f):
        with jax.named_scope("flip"):
            for u in range(users):
                for j in range(events // PAIR):
                    t_buf[f, u, j] = buf[f, u, j * PAIR:(j + 1) * PAIR].T

    def flipped(f, u):
        return jnp.concatenate([t_buf[f, u, j] for j in range(events // PAIR)], axis=1)

    def wide(buf, f, u, tile):
        return jnp.concatenate([buf[f, u, h, tile] for h in range(pieces)], axis=1)

    def prepare(f):
        for i, buf in enumerate((k_buf, v_buf)):
            load_copy(i, f).wait()

            def split(g, carry):
                at = pl.ds(pl.multiple_of(g * SPLIT, SPLIT), SPLIT)
                mixed[...] = raw[i, lax.rem(f, 2), at].astype(F32).reshape(SPLIT * users, PAIR)
                for u in range(users):
                    buf[f, u, at] = mixed[pl.ds(u, SPLIT, users), :].astype(BF16)
                return carry

            with jax.named_scope("split"):
                lax.fori_loop(0, events // SPLIT, split, 0)

            @pl.when(f + 2 < chunks)
            def _():
                load_copy(i, f + 2).start()

        flip(v_buf, f)

    def forward(f, carry):
        with jax.named_scope("wait_queries"):
            arrive(0, f)
        with jax.named_scope("spread_queries"):
            spread(lambda p, s: recvs[0, f, p, s], slot_hold, q_dense.at[f])
        with jax.named_scope("attend"):
            for u in range(users):
                query = split_heads(q_dense[f, u])
                for j in range(0, events, TILE):
                    score = dot(k_buf[f, u, j:j + TILE], query, NT)
                    up = 1.0 + jnp.tanh(score).astype(BF16)
                    weight = score.astype(BF16) * up
                    for h in range(pieces):
                        w_buf[f, u, h, j:j + TILE] = weight[:, lanes(h)]
                        s_buf[f, u, h, j:j + TILE] = up[:, lanes(h)]
            for u in range(users):
                a_dense[f, u] = join_heads(
                    dot(flipped(f, u), wide(w_buf, f, u, slice(None)), NN).astype(BF16)
                ).reshape(n, rows, PAIR)
        with jax.named_scope("send_attended"):
            exchange(1, f, lambda u, c: a_dense[f, u, c], user_hold)
        return carry

    def slopes(f):
        with jax.named_scope("slopes"):
            for u in range(users):
                for h in range(pieces):
                    for j in range(0, events, PAIR):
                        tile = slice(j, j + PAIR)
                        up, weight = s_buf[f, u, h, tile], w_buf[f, u, h, tile]
                        s_buf[f, u, h, tile] = up + weight * (2.0 - up)

    lane_a = lax.broadcasted_iota(jnp.int32, (PAIR, PAIR), 0) // HEAD_DIM
    lane_b = lax.broadcasted_iota(jnp.int32, (PAIR, PAIR), 1) // HEAD_DIM

    def middle(f, carry):
        averager = jnp.where(lane_a == lane_b, 1.0 / HEAD_DIM, 0.0).astype(BF16)

        def head_mean(x):
            high = x.astype(BF16)
            low = (x - high.astype(F32)).astype(BF16)
            return dot(high, averager, NN) + dot(low, averager, NN)

        with jax.named_scope("wait_attended"):
            arrive(1, f)
        with jax.named_scope("middle"):
            attended = gathered(1, f, slot_own)
            gate = small[1, f].reshape(users * rows, PAIR).astype(F32)
            grad = small[2, f].reshape(users * rows, PAIR).astype(F32)
            root = lax.rsqrt(head_mean(attended * attended) + EPS)
            normed = attended * root
            logistic = jax.nn.sigmoid(gate)
            gate_silu = gate * logistic
            slope = logistic * (1.0 + gate * (1.0 - logistic))
            shape = (users, rows, PAIR)
            small_out[0, f] = (normed * gate_silu).astype(BF16).reshape(shape)
            small_out[2, f] = (grad * normed * slope).astype(BF16).reshape(shape)
            grad_normed = grad * gate_silu
            back = root * (grad_normed - normed * head_mean(grad_normed * normed))
            d_own[f] = back.astype(BF16).reshape(shape)
            exchange(2, f, lambda u, c: d_own[f, u], user_own)
        return carry

    def backward(f, carry):
        with jax.named_scope("wait_grads"):
            arrive(2, f)
        with jax.named_scope("spread_grads"):
            spread(lambda p, s: recvs[2, f, p, s], slot_hold, d_dense.at[f])
        with jax.named_scope("query_grads"):
            grads_of = [split_heads(d_dense[f, u]) for u in range(users)]
            grad_scores = [[] for _ in range(users)]
            for j in range(0, events, TILE):
                for u in range(users):
                    grad_weight = dot(v_buf[f, u, j:j + TILE], grads_of[u], NT).astype(BF16)
                    grad_score = grad_weight * wide(s_buf, f, u, slice(j, j + TILE))
                    grad_scores[u].append(grad_score)
                    for h in range(pieces):
                        s_buf[f, u, h, j:j + TILE] = grad_score[:, lanes(h)]
            for u in range(users):
                a_dense[f, u] = join_heads(
                    (dot(flipped(f, u), jnp.concatenate(grad_scores[u], axis=0), NN)
                     * 0.0625).astype(BF16)
                ).reshape(n, rows, PAIR)
        with jax.named_scope("send_query_grads"):
            exchange(3, f, lambda u, c: a_dense[f, u, c], user_hold)
        return carry

    def event_grads(f, carry):
        with jax.named_scope("event_grads"):
            for u in range(users):
                query = split_heads(q_dense[f, u])
                grad = split_heads(d_dense[f, u])
                for j in range(0, events, TILE):
                    tile = slice(j, j + TILE)
                    v_buf[f, u, tile] = dot(wide(w_buf, f, u, tile), grad, NN).astype(BF16)
                    k_buf[f, u, tile] = dot(wide(s_buf, f, u, tile), query, NN).astype(BF16)
        return carry

    def finish(f, carry):
        with jax.named_scope("wait_query_grads"):
            arrive(3, f)
        with jax.named_scope("finish"):
            small_out[1, f] = gathered(3, f, slot_own).astype(BF16).reshape(users, rows, PAIR)
        return carry

    prepare(0)
    with jax.named_scope("barrier"):
        pl.semaphore_wait(barrier, n - 1)
    for p in range(n):
        stage[p, SLOTS] = jnp.zeros((rows, PAIR), BF16)

    def send_queries(f, carry):
        exchange(0, f, lambda u, c: small[0, f, u], user_own)
        return carry

    def opening(f, carry):
        prepare(f)
        return carry

    def between(f, carry):
        middle(f, carry)

        @pl.when(f + early < chunks)
        def _():
            flip(k_buf, f + early)

        slopes(f)
        return carry

    early = min(2, chunks)

    def flip_early(f, carry):
        flip(k_buf, f)
        return carry

    with jax.named_scope("send_queries"):
        lax.fori_loop(0, chunks, send_queries, 0)
    lax.fori_loop(0, n, functools.partial(tables, False), 0)
    sort_users(1)
    sort_users(2)
    lax.fori_loop(1, chunks, opening, 0)
    lax.fori_loop(0, chunks, forward, 0)
    lax.fori_loop(0, early, flip_early, 0)
    lax.fori_loop(0, chunks, between, 0)
    lax.fori_loop(0, chunks, backward, 0)
    lax.fori_loop(0, chunks, event_grads, 0)
    lax.fori_loop(0, chunks, finish, 0)
    with jax.named_scope("drain"):
        for ph in range(4):
            sent(ph)


def lay_out(small_in, dkeys, dvalues, layer_out, grad_queries, grad_gate, out_keys, out_values,
            joined, tiny, sem, tiny_sem):
    chunks, users, events = dkeys.shape[:3]
    depth = joined.shape[0]
    blocks = [(i, j) for j in range(0, events, MERGE) for i in range(2)]

    def store(at):
        i, j = blocks[at]
        return pltpu.make_async_copy(
            joined.at[at % depth], (out_keys, out_values)[i].at[pl.ds(j, MERGE)], sem.at[at % depth])

    def store_tiny(i):
        return pltpu.make_async_copy(
            tiny.at[i], (layer_out, grad_queries, grad_gate)[i], tiny_sem.at[i])

    for at, (i, j) in enumerate(blocks):
        if at >= depth:
            store(at - depth).wait()
        for f in range(chunks):
            parts = [(dkeys, dvalues)[i][f, u, j:j + MERGE] for u in range(users)]
            joined[at % depth, :, :, lanes(f)] = jnp.concatenate(parts, axis=1).reshape(
                MERGE, users, PAIR)
        store(at).start()
        if at == 2:
            for k in range(3):
                for f in range(chunks):
                    tiny[k, :, :, lanes(f)] = jnp.swapaxes(small_in[k, f], 0, 1)
                store_tiny(k).start()
    for k in range(3):
        store_tiny(k).wait()
    for at in range(max(0, len(blocks) - depth), len(blocks)):
        store(at).wait()


def body(n, queries, gate_pre, event_keys, event_values, block_lists, history_len, out_grad):
    rows, users, width = queries.shape
    events = event_keys.shape[0]
    chunks = width // PAIR
    latents = n * rows
    vmem = pl.BlockSpec(memory_space=pltpu.VMEM)
    hbm = pl.BlockSpec(memory_space=pl.ANY)
    table = [pltpu.SMEM((n, SLOTS), jnp.int32), pltpu.SMEM((n, users), jnp.int32)]
    flops = 6 * 2 * users * width * latents * events
    lists = block_lists.transpose(1, 2, 0)
    packed = (chunks, users, events, PAIR)
    dense = (chunks, users, latents, PAIR)
    square = (chunks, users, 2 * latents // PAIR, events, PAIR)
    outs = (pltpu.VMEM((3, chunks, users, rows, PAIR), BF16), pltpu.VMEM(packed, BF16),
            pltpu.VMEM(packed, BF16))
    kept = pl.pallas_call(
        functools.partial(kernel, n, chunks),
        out_shape=outs,
        in_specs=[hbm] * 7,
        out_specs=(vmem,) * len(outs),
        scratch_shapes=[
            pltpu.SMEM(lists.shape, jnp.int32),
            pltpu.SMEM(history_len.shape, jnp.int32),
            pltpu.VMEM((3, rows, users, width), BF16),
            pltpu.VMEM((2, 2, events, users, PAIR), BF16),
            pltpu.VMEM((SPLIT * users, PAIR), F32),
            pltpu.VMEM((3, chunks, users, rows, PAIR), BF16),
            pltpu.VMEM((chunks, users, events // PAIR, PAIR, PAIR), BF16),
            pltpu.VMEM(square, BF16),
            pltpu.VMEM(square, BF16),
            pltpu.VMEM(dense, BF16),
            pltpu.VMEM(dense, BF16),
            pltpu.VMEM((chunks, users, n, rows, PAIR), BF16),
            pltpu.VMEM((chunks, users, rows, PAIR), BF16),
            pltpu.VMEM((n, SLOTS + 1, rows, PAIR), BF16),
            pltpu.VMEM((4, chunks, n, SLOTS, rows, PAIR), BF16),
            pltpu.VMEM((4, chunks, n, SLOTS, rows, PAIR), BF16),
            *table,
            *table,
            pltpu.SemaphoreType.DMA((4,)),
            pltpu.SemaphoreType.DMA((4, chunks)),
            pltpu.SemaphoreType.DMA((2, chunks)),
            pltpu.SemaphoreType.DMA((5,)),
        ],
        compiler_params=pltpu.CompilerParams(
            collective_id=0, has_side_effects=True, vmem_limit_bytes=54 * 1024 * 1024
        ),
        cost_estimate=pl.CostEstimate(
            flops=flops, bytes_accessed=8 * users * events * width, transcendentals=0),
        name="sparse_attention",
    )(*(pltpu.with_memory_space_constraint(x, pltpu.HBM) for x in (
        lists, history_len, queries, gate_pre, out_grad, event_keys, event_values)))

    tiny = jax.ShapeDtypeStruct((rows, users, width), BF16)
    large = jax.ShapeDtypeStruct((events, users, width), BF16)
    return pl.pallas_call(
        lay_out,
        out_shape=(tiny, tiny, tiny, large, large),
        in_specs=[vmem] * len(outs),
        out_specs=(hbm,) * 5,
        scratch_shapes=[
            pltpu.VMEM((4, MERGE, users, width), BF16),
            pltpu.VMEM((3, rows, users, width), BF16),
            pltpu.SemaphoreType.DMA((4,)),
            pltpu.SemaphoreType.DMA((3,)),
        ],
        compiler_params=pltpu.CompilerParams(vmem_limit_bytes=16 * 1024 * 1024),
        cost_estimate=pl.CostEstimate(
            flops=0, bytes_accessed=8 * users * events * width, transcendentals=0),
        name="lay_out",
    )(*(pltpu.with_memory_space_constraint(x, pltpu.VMEM) for x in kept))


def solution(mesh):
    shard = P("seq", "dp", "head")
    return jax.shard_map(
        functools.partial(body, mesh.shape["seq"]),
        mesh=mesh,
        in_specs=(shard, shard, shard, shard, P(None, "dp", None), P("dp"), shard),
        out_specs=(shard,) * 5,
        check_vma=False,
    )
```
